32 devices in a mesh: gx: 4 (over z), gy: 2 (over x), gz: 4 (over y, core).
Axes of the slice: x: 2, y: 2, z: 4, core: 2. Of those that a mesh axis runs over, the one named last changes fastest.
Arguments:
- initial_field: float32 [3, 32, 64, 512], P(None, 'gx', 'gy', 'gz'), may hold values from -6 to 6
- inv_permittivity: float32 [32, 64, 512], P('gx', 'gy', 'gz'), may hold values from 0.25 to 1
- history: bfloat16 [768, 12, 256], P(('gx', 'gy', 'gz')), may hold values from -6 to 6
- tile_rows: int32 [768], P(('gx', 'gy', 'gz')), may hold values from 0 to 255
- owners: int32 [768, 1], P(('gx', 'gy', 'gz')), may hold values from 0 to 3; in each aligned block of 24 rows (0 to 23, 24 to 47, ...) at most 12 rows name the same one
- delays: int32 [768, 4096], P(('gx', 'gy', 'gz')), may hold values from 0 to 3
- weights: bfloat16 [256, 4096], replicated, may hold values from -0.375 to 0.375
Outputs:
- efield: float32 [3, 32, 64, 512], P(None, 'gx', 'gy', 'gz')
- far_field: float32 [4, 20, 4096], P('gx', None, ('gy', 'gz'))
The draws below stay inside these ranges and needn't reach their ends.
Inputs may be any that keep to these rules, and one draw needn't show every extreme that they name: `owners`: among the 24 tiles of one device no section is named more than 12 times, a bound that some block reaches.
All inputs are finite; a program needn't handle non-finite values.
Results may differ from the reference program's by a relative error of at most 0.0014.
Values may be sent and summed in bfloat16 or wider, within the bound.
A program may use at most 128 MiB of HBM per device.

```python
import math
import jax
import jax.numpy as jnp
import numpy as np
from jax import lax

CX = 8
CY = 32
CZ = 128
STEPS = 4
HIST = 16
LAG = 4
DIRS = 4096
FT = 24
CAP = 12
HPAST = 12
NB = 20
NX = 32
NY = 64
NZ = 512
TILES = 768
N_GX = 4
N_GY = 2
N_GZ = 4


def touch_ends(drawn, key, low, largest):
    dims = drawn.shape
    spot = [jax.random.randint(jax.random.fold_in(key, axis), (), 0, dims[axis]) for axis in range(len(dims))]
    drawn = drawn.at[tuple(spot)].set(low)
    longest = dims.index(max(dims))
    spot[longest] = (spot[longest] + 1) % dims[longest]
    return drawn.at[tuple(spot)].set(largest)


def steps_of(stream_key, extent, shards, least, high):
    gain = 1.0
    for position, shards_of in shards:
        steps = jax.random.uniform(jax.random.fold_in(jax.random.fold_in(stream_key, 6), position), (shards_of,), jnp.float32, least / len(shards), high / len(shards))
        gain = gain * jnp.repeat(jnp.exp(steps), extent[position] // shards_of).reshape((-1,) + (1,) * (len(extent) - 1 - position))
    return gain


def shared_out(key, own, number, rows, amount, top, reach, skew):
    order = jax.random.permutation(key, amount)
    heavy_load, usual = load_shares(amount, rows * top, reach, skew, True), load_shares(amount, rows * top, reach, skew, False)
    places = jnp.arange(amount)

    def named(tallies, rotation):
        used = int((tallies > 0).sum())
        fixed = max(1, used // 4)
        moved = fixed + (places - fixed + rotation * (used - fixed)) % max(1, amount - fixed)
        return jnp.zeros((amount,), jnp.int32).at[order[jnp.where(places < fixed, places, moved)]].set(jnp.asarray(tallies, jnp.int32))

    tallies = jnp.where(number % 4 == 0, named(heavy_load, number // 4), named(usual, number - number // 4 - 1))
    mixed = jax.random.permutation(jax.random.fold_in(own, 3), amount)
    giver, sink = mixed[0:amount // 2 * 2:2], mixed[1:amount // 2 * 2:2]
    margin = jnp.minimum(tallies[giver] - 1, reach - tallies[sink]) // 2
    margin = jnp.where((giver == order[0]) | (sink == order[0]) | (tallies[sink] == 0), 0, jnp.maximum(margin, 0))
    moved = jax.random.randint(jax.random.fold_in(own, 4), (amount // 2,), 0, 1 << 20) % (margin + 1)
    tallies = tallies.at[giver].add(-moved).at[sink].add(moved)
    items = jnp.searchsorted(jnp.cumsum(tallies), jnp.arange(rows * top), side="right").astype(jnp.int32)
    grid = items.reshape(top, rows).T
    grid = grid[jax.random.permutation(jax.random.fold_in(own, 1), rows)]
    rotation = jax.random.randint(jax.random.fold_in(own, 2), (rows, 1), 0, top)
    return jnp.take_along_axis(grid, (jnp.arange(top)[None, :] + rotation) % top, axis=1)


def load_shares(amount, total, bound, lean, full):
    weights = [(1 << 20) // math.isqrt(standing ** lean) + 1 for standing in range(1, amount + 1)]
    largest = bound if full else min(bound, max(-(-total // amount), total * weights[0] // sum(weights)))
    least = 1 if total - largest >= amount - 1 else 0
    holding, spare = [largest] + [least] * (amount - 1), total - largest - least * (amount - 1)
    while spare > 0:
        movable = [i for i in range(1, amount) if holding[i] < largest] or [i for i in range(1, amount) if holding[i] < bound]
        whole, budget = sum([weights[i] for i in movable]), spare
        for i in movable:
            addition = min(bound - holding[i], max(1, budget * weights[i] // whole), spare)
            holding[i] = holding[i] + addition
            spare = spare - addition
    return np.array(holding)


def scatter_about(rng, shape, spread, limit, cuts=(), held_as=jnp.bfloat16):
    entries = jax.random.normal(rng, shape, jnp.float32) * spread
    if len(cuts) > 0:
        entries = steps_of(rng, shape, cuts, -0.22, 0.18) * entries
    return jnp.clip(entries, min=-limit, max=limit).astype(held_as)


def setup_inputs(seed: int = 0) -> dict:
    keys = jax.random.split(jax.random.key(seed), 8)
    initial_field = scatter_about(keys[0], (3, NX, NY, NZ), 1.0, 6.0, ((1, 4), (2, 2), (3, 4)), jnp.float32)
    inv_permittivity = jnp.clip(jnp.exp(math.log(1.0) - 1.3862944 * jax.random.uniform(keys[1], (NX, NY, NZ), jnp.float32) ** steps_of(keys[1], (NX, NY, NZ), ((0, 4), (1, 2), (2, 4)), -0.2, 0.2)), 0.25, 1.0)
    history = scatter_about(keys[2], (TILES, HPAST, 2 * CZ), 1.0, 6.0, ((0, 32),))
    tile_rows = touch_ends(jax.random.randint(keys[3], (TILES,), 0, CX * CY), jax.random.fold_in(keys[3], 1), 0, (CX * CY) - 1).astype(jnp.int32)
    owners_keys = jax.random.split(jax.random.fold_in(keys[4], 1), TILES // FT)
    owners_turns = jax.random.permutation(jax.random.fold_in(keys[4], 3), TILES // FT)
    owners = jax.vmap(lambda own, number: shared_out(jax.random.fold_in(keys[4], 2), own, number, FT, N_GX, 1, CAP, 2))(owners_keys, owners_turns).reshape((TILES, 1))
    delays = touch_ends(jax.random.randint(keys[5], (TILES, DIRS), 0, LAG), jax.random.fold_in(keys[5], 1), 0, LAG - 1).astype(jnp.int32)
    weights = scatter_about(keys[6], (2 * CZ, DIRS), (2 * CZ) ** -0.5, 0.375)
    return dict(initial_field=initial_field, inv_permittivity=inv_permittivity, history=history, tile_rows=tile_rows, owners=owners, delays=delays, weights=weights)


courant = 0.5


def curl_upper(padded):
    base = padded[:, :-1, :-1, :-1]
    along_x = padded[:, 1:, :-1, :-1] - base
    along_y = padded[:, :-1, 1:, :-1] - base
    along_z = padded[:, :-1, :-1, 1:] - base
    return jnp.stack([along_y[2] - along_z[1], along_z[0] - along_x[2], along_x[1] - along_y[0]])


def curl_lower(padded):
    base = padded[:, 1:, 1:, 1:]
    along_x = base - padded[:, :-1, 1:, 1:]
    along_y = base - padded[:, 1:, :-1, 1:]
    along_z = base - padded[:, 1:, 1:, :-1]
    return jnp.stack([along_y[2] - along_z[1], along_z[0] - along_x[2], along_x[1] - along_y[0]])


def shifted(proj, delay_block):
    padded = jnp.pad(proj, ((0, 0), (0, NB - HIST), (0, 0)))
    times = lax.broadcasted_iota(jnp.int32, (1, NB, 1), 1)
    where_from = (times - delay_block[:, None, :]) % NB
    return jnp.take_along_axis(padded, where_from, axis=1)


def reference(initial_field, inv_permittivity, history, tile_rows, owners, delays, weights):
    efield = initial_field
    magnetic = jnp.zeros_like(initial_field)
    group = N_GY * N_GZ
    device = jnp.arange(TILES, dtype=jnp.int32) // FT
    block_x = device // group
    block_y = (device // N_GZ) % N_GY
    block_z = device % N_GZ
    global_x = block_x * CX + tile_rows // CY
    global_y = block_y * CY + tile_rows % CY
    samples = []
    for step_index in range(STEPS):
        upper = jnp.pad(efield, ((0, 0), (0, 1), (0, 1), (0, 1)))
        magnetic = magnetic - courant * curl_upper(upper)
        split = magnetic[:2].reshape(2, NX, NY, N_GZ, CZ)
        picked = split[:, global_x, global_y, block_z, :]
        samples.append(jnp.transpose(picked, (1, 0, 2)).reshape(TILES, 2 * CZ))
        lower = jnp.pad(magnetic, ((0, 0), (1, 0), (1, 0), (1, 0)))
        efield = efield + courant * inv_permittivity * curl_lower(lower)
    recent = jnp.stack(samples, axis=1).astype(jnp.bfloat16)
    full_history = jnp.concatenate([history, recent], axis=1)
    weights_wide = weights.astype(jnp.float32)
    blocks = TILES // FT

    def one_block(total, pieces):
        block_history, block_delays, block_owners = pieces
        proj = jnp.einsum('ktf,fd->ktd', block_history.astype(jnp.float32), weights_wide)
        moved = shifted(proj, block_delays)
        return total + jax.ops.segment_sum(moved, block_owners[:, 0], num_segments=N_GX), None

    start = jnp.zeros((N_GX, NB, DIRS), jnp.float32)
    far, _ = lax.scan(one_block, start, (full_history.reshape(blocks, FT, HIST, 2 * CZ), delays.reshape(blocks, FT, DIRS), owners.reshape(blocks, FT, 1)))
    scale = (TILES / N_GX) ** -0.5
    return efield, far * scale
```

```python
import functools

import jax
import jax.numpy as jnp
from jax import lax
from jax.experimental import pallas as pl
from jax.experimental.pallas import tpu as pltpu
from jax.sharding import PartitionSpec as P

STEPS = 4
LAG = 4
NB = 20

courant = 0.5
MESH = pl.DeviceIdType.MESH
WIDE = 256


def kernel(
    dims,
    field_ref, perm_ref, hist_hbm, rows_hbm, owners_hbm, delays_hbm, weights_hbm,
    e, far_ref,
    h, perm, hist_ref, rows_ref, owners_ref, delays_ref, weights_ref,
    xs, ys, zs, xt, yt, zt,
    xr, yr, zr, xl, yl, zl, exz, eyz, exy, ezy, eyx, ezx,
    hxm, hym, hzm,
    placed_past, placed_new, placed_delay, proj,
    part_old, part_new, recv_a_old, recv_a_new, sum_a_old, sum_a_new,
    recv_b_old, recv_b_new, sum_b_old, sum_b_new, recv_c_old, recv_c_new,
    hs_sem, hr_sem, a_send, a_recv, b_send, b_recv, c_send, c_recv, in_sem,
):
    n_x, n_y, n_z, sx, sy, sz, tiles, hpast, cap, old_rows, new_rows, share = dims
    gx, gy, gz = lax.axis_index("gx"), lax.axis_index("gy"), lax.axis_index("gz")
    core, plane_z = gz % 2, gz // 2
    plane_n = n_y * (n_z // 2)
    plane_me = gy * (n_z // 2) + plane_z
    slots = n_x * cap
    wide_rows = max(8, n_x)
    groups = slots // wide_rows
    members = n_y * n_z

    loads = [
        pltpu.make_async_copy(source, target, in_sem.at[i])
        for i, (source, target) in enumerate(
            (
                (field_ref, e), (owners_hbm, owners_ref), (rows_hbm, rows_ref), (hist_hbm, hist_ref),
                (delays_hbm, delays_ref), (perm_ref, perm), (weights_hbm, weights_ref),
            )
        )
    ]
    for load in loads:
        load.start()

    for ref in (xr, yr, zr, xl, yl, zl, exz, eyz, exy, ezy, eyx, ezx):
        ref[...] = jnp.zeros_like(ref)

    barrier = pltpu.get_barrier_semaphore()
    for j in range(1, n_x):
        pl.semaphore_signal(barrier, inc=1, device_id=((gx + j) % n_x, gy, gz), device_id_type=MESH)
    member_me = gy * n_z + gz
    for j in range(1, members):
        other = (member_me + j) % members
        pl.semaphore_signal(
            barrier, inc=1, device_id=(gx, other // n_z, other % n_z), device_id_type=MESH
        )

    tail = slice(sy - 8, sy)
    copies = (
        ((-1, 0, 0), lambda k: xs.at[k], lambda k: xr.at[k]),
        ((1, 0, 0), lambda k: xt.at[k], lambda k: xl.at[k]),
        ((1, 0, -1), lambda k: zs.at[k], lambda k: exz.at[k]),
        ((-1, 0, 1), lambda k: xs.at[k, 1], lambda k: ezx.at[k]),
        ((1, -1, 0), lambda k: ys.at[k], lambda k: exy.at[k]),
        ((-1, 1, 0), lambda k: xs.at[k, 0, tail], lambda k: eyx.at[k]),
        ((0, 1, -1), lambda k: zs.at[k, tail], lambda k: eyz.at[k]),
        ((0, -1, 1), lambda k: ys.at[k], lambda k: ezy.at[k]),
        ((0, -1, 0), lambda k: ys.at[k], lambda k: yr.at[k]),
        ((0, 1, 0), lambda k: yt.at[k], lambda k: yl.at[k]),
        ((0, 0, -1), lambda k: zs.at[k], lambda k: zr.at[k]),
        ((0, 0, 1), lambda k: zt.at[k], lambda k: zl.at[k]),
    )

    def at_offset(offset, sign):
        inside, place = None, []
        for pos, count, step in zip((gx, gy, gz), (n_x, n_y, n_z), offset):
            step = sign * step
            if step:
                fits = (pos > 0) if step < 0 else (pos < count - 1)
                inside = fits if inside is None else jnp.logical_and(inside, fits)
            place.append(jnp.clip(pos + step, 0, count - 1) if step else pos)
        return inside, tuple(place)

    diagonals = ((1, 0, -1), (-1, 0, 1), (1, -1, 0), (-1, 1, 0))
    for ox, oy, oz in diagonals:
        target = ((gx + ox + n_x) % n_x, (gy + oy + n_y) % n_y, (gz + oz + n_z) % n_z)
        pl.semaphore_signal(barrier, inc=1, device_id=target, device_id_type=MESH)

    lane = lax.broadcasted_iota(jnp.int32, (sy, sz), 1)
    row = lax.broadcasted_iota(jnp.int32, (sy, sz), 0)

    def stage(slot):
        for i, c in enumerate((1, 2)):
            xs[slot, i] = e[c, 0]
        for c in range(3):
            xt[slot, c] = e[c, sx - 1]
        for i, c in enumerate((0, 2)):
            for x in range(sx):
                ys[slot, i, x : x + 1, :] = e[c, x, 0:1, :]
        for c in range(3):
            for x in range(sx):
                yt[slot, c, x : x + 1, :] = e[c, x, sy - 1 : sy, :]
        low = jnp.zeros((sy, sz), jnp.float32)
        high = jnp.zeros((sy, sz), jnp.float32)
        for c in range(3):
            for x in range(sx):
                at = c * sx + x
                if c < 2:
                    low = jnp.where(lane == at, pltpu.roll(e[c, x], at, 1), low)
                high = jnp.where(lane == at, pltpu.roll(e[c, x], at + 1, 1), high)
        zs[slot] = low
        zt[slot] = high

    def halo_copy(slot, number):
        offset, source, target = copies[number]
        return pltpu.make_async_remote_copy(
            src_ref=source(slot), dst_ref=target(slot),
            send_sem=hs_sem.at[slot, number], recv_sem=hr_sem.at[slot, number],
            device_id=at_offset(offset, 1)[1], device_id_type=MESH,
        )

    def send_halo(slot):
        for number in range(len(copies)):
            @pl.when(at_offset(copies[number][0], 1)[0])
            def _():
                halo_copy(slot, number).start()

    def wait_halo(slot):
        for number in range(len(copies)):
            @pl.when(at_offset(copies[number][0], -1)[0])
            def _():
                halo_copy(slot, number).wait_recv()

    def end_halo(slot):
        for number in range(len(copies)):
            @pl.when(at_offset(copies[number][0], 1)[0])
            def _():
                halo_copy(slot, number).wait_send()

    def next_y(v, slot, i, x, low):
        if low:
            return jnp.where(row == 0, hym[i, x : x + 1, :], pltpu.roll(v, 1, 0))
        return jnp.where(row == sy - 1, yr[slot, i, x : x + 1, :], pltpu.roll(v, sy - 1, 0))

    def next_z(v, c, x, packed, low):
        if low:
            return jnp.where(
                lane == 0, pltpu.roll(hzm[c], (sz - x) % sz, 1), pltpu.roll(v, 1, 1)
            )
        at = c * sx + x
        return jnp.where(
            lane == sz - 1, pltpu.roll(packed, (sz - 1 - at) % sz, 1), pltpu.roll(v, sz - 1, 1)
        )

    def next_x(ref, slot, i, c, x, low):
        if low:
            return ref[c, x - 1] if x > 0 else hxm[i]
        return ref[c, x + 1] if x < sx - 1 else xr[slot, i]

    lane8 = lax.broadcasted_iota(jnp.int32, (sx, sz), 1)
    row8 = lax.broadcasted_iota(jnp.int32, (sx, sz), 0)

    def update_below(slot, first):
        def put(ref, i, change, exists):
            fresh = -change if first else ref[i] - change
            ref[i] = jnp.where(exists, fresh, 0.0)

        ex, ey, ez = xl[slot, 0], xl[slot, 1], xl[slot, 2]
        ex_z = jnp.where(
            lane == sz - 1, pltpu.roll(exz[slot], sz - sx, 1), pltpu.roll(ex, sz - 1, 1)
        )
        ex_y = jnp.where(row == sy - 1, exy[slot, 0, sx - 1 : sx, :], pltpu.roll(ex, sy - 1, 0))
        put(hxm, 0, courant * ((ex_z - ex) - (xs[slot, 1] - ez)), gx > 0)
        put(hxm, 1, courant * ((xs[slot, 0] - ey) - (ex_y - ex)), gx > 0)

        ex, ey, ez = yl[slot, 0], yl[slot, 1], yl[slot, 2]
        edge = jnp.sum(
            jnp.where(lane8 == row8 + sx, jnp.broadcast_to(eyz[slot, 7:8, :], (sx, sz)), 0.0),
            axis=1, keepdims=True,
        )
        ey_z = jnp.where(lane8 == sz - 1, edge, pltpu.roll(ey, sz - 1, 1))
        ey_x = jnp.where(row8 == sx - 1, eyx[slot, 7:8, :], pltpu.roll(ey, sx - 1, 0))
        put(hym, 0, courant * ((ys[slot, 1] - ez) - (ey_z - ey)), gy > 0)
        put(hym, 1, courant * ((ey_x - ey) - (ys[slot, 0] - ex)), gy > 0)

        ex = zl[slot]
        ey = pltpu.roll(ex, sz - sx, 1)
        ez = pltpu.roll(ex, sz - 2 * sx, 1)
        ex_up = zs[slot]
        ey_up = pltpu.roll(ex_up, sz - sx, 1)
        column = jnp.sum(jnp.where(lane8 == sz - 1, ezy[slot, 1], 0.0), axis=1, keepdims=True)
        edge = jnp.sum(jnp.where(lane8 == row8, column, 0.0), axis=0, keepdims=True)
        ez_y = jnp.where(row == sy - 1, edge, pltpu.roll(ez, sy - 1, 0))
        ez_x = jnp.where(lane == sx - 1, pltpu.roll(ezx[slot], sx, 1), pltpu.roll(ez, sz - 1, 1))
        put(hzm, 0, courant * ((ez_y - ez) - (ey_up - ey)), gz > 0)
        put(hzm, 1, courant * ((ex_up - ex) - (ez_x - ez)), gz > 0)

    def update_h(slot, first):
        packed = zr[slot]
        for x in range(sx):
            ex, ey, ez = e[0, x], e[1, x], e[2, x]
            ez_y, ex_y = next_y(ez, slot, 1, x, False), next_y(ex, slot, 0, x, False)
            ey_z, ex_z = next_z(ey, 1, x, packed, False), next_z(ex, 0, x, packed, False)
            ez_x, ey_x = next_x(e, slot, 1, 2, x, False), next_x(e, slot, 0, 1, x, False)
            changes = (
                courant * ((ez_y - ez) - (ey_z - ey)),
                courant * ((ex_z - ex) - (ez_x - ez)),
                courant * ((ey_x - ey) - (ex_y - ex)),
            )
            for c in range(3):
                h[c, x] = -changes[c] if first else h[c, x] - changes[c]

    def update_e(slot):
        for x in range(sx):
            hx, hy, hz = h[0, x], h[1, x], h[2, x]
            hz_y, hx_y = next_y(hz, slot, 1, x, True), next_y(hx, slot, 0, x, True)
            hy_z, hx_z = next_z(hy, 1, x, None, True), next_z(hx, 0, x, None, True)
            hz_x, hy_x = next_x(h, slot, 1, 2, x, True), next_x(h, slot, 0, 1, x, True)
            scale = courant * perm[x]
            e[0, x] = e[0, x] + scale * ((hz - hz_y) - (hy - hy_z))
            e[1, x] = e[1, x] + scale * ((hx - hx_z) - (hz - hz_x))
            e[2, x] = e[2, x] + scale * ((hy - hy_x) - (hx - hx_y))

    loads[0].wait()
    stage(0)

    loads[1].wait()
    loads[2].wait()
    owner_row = owners_ref[...]
    ti = lax.broadcasted_iota(jnp.int32, (tiles, tiles), 0)
    tj = lax.broadcasted_iota(jnp.int32, (tiles, tiles), 1)
    owner_wide = jnp.broadcast_to(owner_row, (tiles, tiles))
    owner_col = jnp.sum(jnp.where(ti == tj, owner_wide, 0), axis=1, keepdims=True)
    rank_row = jnp.sum(
        jnp.where((owner_col == owner_wide) & (ti < tj), 1, 0), axis=0, keepdims=True
    )
    slot_row = rank_row * n_x + owner_row
    slot_ids = lax.broadcasted_iota(jnp.int32, (slots, tiles), 0)
    place = jnp.where(slot_ids == slot_row, 1.0, 0.0).astype(jnp.bfloat16)
    pick = jnp.where(
        lax.broadcasted_iota(jnp.int32, (sx * sy, tiles), 0) == rows_ref[...], 1.0, 0.0
    ).astype(jnp.bfloat16)
    sampler = lax.dot_general(
        place, pick, (((1,), (1,)), ((), ())), preferred_element_type=jnp.float32
    ).astype(jnp.bfloat16)

    pl.semaphore_wait(barrier, n_x - 1 + members - 1 + len(diagonals))
    send_halo(0)

    loads[3].wait()
    for t in range(hpast):
        placed_past[t * slots : (t + 1) * slots, :] = jnp.dot(
            place, hist_ref[t], preferred_element_type=jnp.float32
        ).astype(jnp.bfloat16)
    loads[4].wait()
    placed_delay[...] = jnp.dot(
        place, delays_ref[...].astype(jnp.float32).astype(jnp.bfloat16),
        preferred_element_type=jnp.float32,
    )
    loads[5].wait()
    loads[6].wait()

    def project(source, time0, times, part, pad_rows, add, parity, first, count):
        per = share // WIDE

        def body(i, carry):
            member = 2 * (i // per) + parity
            start = pl.multiple_of(member * share + (i % per) * WIDE, WIDE)
            proj[0 : times * slots, :] = jnp.dot(
                source[time0 * slots : (time0 + times) * slots, :], weights_ref[:, pl.ds(start, WIDE)],
                preferred_element_type=jnp.float32,
            )
            for q in range(WIDE // 128):
                column = pl.multiple_of(start + q * 128, 128)
                inside = (i % per) * (WIDE // 128) + q
                for block in range(wide_rows // 8):
                    bins = [None] * (time0 + times + LAG - 1)
                    for g in range(groups):
                        base = g * wide_rows + block * 8
                        late = placed_delay[base : base + 8, pl.ds(column, 128)]
                        keeps = [late == float(lag) for lag in range(LAG)]
                        for t in range(times):
                            value = proj[t * slots + base : t * slots + base + 8, q * 128 : q * 128 + 128]
                            for lag in range(LAG):
                                piece = jnp.where(keeps[lag], value, 0.0)
                                b = time0 + t + lag
                                bins[b] = piece if bins[b] is None else bins[b] + piece
                    bins = bins + [None] * (pad_rows - len(bins))
                    for b in range(pad_rows):
                        if bins[b] is None:
                            if add:
                                continue
                            bins[b] = jnp.zeros((8, 128), jnp.float32)
                        if n_x >= 8:
                            kept, many = bins[b], 8
                        else:
                            kept, many = bins[b][0:n_x], n_x
                            for other in range(n_x, 8, n_x):
                                kept = kept + bins[b][other : other + n_x]
                        spot = pl.ds(block * 8 * pad_rows + b, many, stride=pad_rows)
                        if add:
                            kept = kept + part[member, inside, spot, :]
                        part[member, inside, spot, :] = kept
            return carry

        lax.fori_loop(first, first + count, body, 0)

    sets = (
        (part_old, recv_a_old, sum_a_old, recv_b_old, sum_b_old, recv_c_old, old_rows),
        (part_new, recv_a_new, sum_a_new, recv_b_new, sum_b_new, recv_c_new, new_rows),
    )

    def copy_a(which, m):
        part, recv = sets[which][0], sets[which][1]
        other = 1 - core
        return pltpu.make_async_remote_copy(
            src_ref=part.at[2 * m + other], dst_ref=recv.at[m],
            send_sem=a_send.at[which, m], recv_sem=a_recv.at[which, m],
            device_id=(gx, gy, plane_z * 2 + other), device_id_type=MESH,
        )

    blocks = share // 128
    cuts = ((0, blocks // 2, blocks), (0, blocks))

    def copy_b(which, piece, j):
        span = slice(cuts[which][piece], cuts[which][piece + 1])
        summed, recv = sets[which][2], sets[which][3]
        other = (plane_me + j) % plane_n
        half = n_z // 2
        return pltpu.make_async_remote_copy(
            src_ref=summed.at[other, span], dst_ref=recv.at[j, span],
            send_sem=b_send.at[2 * which + piece, j], recv_sem=b_recv.at[2 * which + piece, j],
            device_id=(gx, other // half, (other % half) * 2 + core), device_id_type=MESH,
        )

    def copy_c(which, j):
        summed, recv, rows = sets[which][4], sets[which][5], sets[which][6]
        other = (gx + j) % n_x
        return pltpu.make_async_remote_copy(
            src_ref=summed.at[:, pl.ds(pl.multiple_of(other * rows, 8), rows)], dst_ref=recv.at[j],
            send_sem=c_send.at[which, j], recv_sem=c_recv.at[which, j],
            device_id=(other, gy, gz), device_id_type=MESH,
        )

    def begin_a(which):
        for m in range(plane_n):
            copy_a(which, m).start()

    def a_to_b(which):
        part, recv, summed = sets[which][0], sets[which][1], sets[which][2]
        for j in list(range(1, plane_n)) + [0]:
            m = (plane_me + j) % plane_n
            copy_a(which, m).wait_recv()
            summed[m] = part[2 * m + core] + recv[m]
            if j > 0:
                copy_b(which, 0, j).start()

    def b_to_c(which):
        total = sets[which][2][plane_me]
        for j in range(1, plane_n):
            for piece in range(len(cuts[which]) - 1):
                copy_b(which, piece, j).wait_recv()
            total = total + sets[which][3][j]
        sets[which][4][...] = total
        for j in range(1, n_x):
            copy_c(which, j).start()

    def end_c(which):
        rows = sets[which][6]
        total = sets[which][4][:, pl.ds(pl.multiple_of(gx * rows, 8), rows), :]
        for j in range(1, n_x):
            copy_c(which, j).wait_recv()
            total = total + sets[which][5][j]
        for m in range(plane_n):
            copy_a(which, m).wait_send()
        for j in range(1, plane_n):
            for piece in range(len(cuts[which]) - 1):
                copy_b(which, piece, j).wait_send()
        for j in range(1, n_x):
            copy_c(which, j).wait_send()
        return total

    chunks = plane_n * share // WIDE
    other = 1 - core

    def sample(step):
        for m in range(2):
            flat = h[m].reshape(sx * sy, sz).astype(jnp.bfloat16)
            placed_new[step * slots : (step + 1) * slots, m * sz : (m + 1) * sz] = jnp.dot(
                sampler, flat, preferred_element_type=jnp.float32
            ).astype(jnp.bfloat16)

    def past(parity, first, count):
        project(placed_past, 0, hpast, part_old, old_rows, False, parity, first, count)

    def early(parity, first, count):
        project(placed_new, 0, STEPS - 1, part_new, new_rows, False, parity, first, count)

    def last(parity):
        project(placed_new, STEPS - 1, 1, part_new, new_rows, True, parity, 0, chunks)

    def beside(step):
        if step == 0:
            past(other, 0, chunks)
            begin_a(0)
            past(core, 0, chunks)
        elif step == 1:
            a_to_b(0)
        elif step == 2:
            for j in range(1, plane_n):
                copy_b(0, 1, j).start()
        elif step == 3:
            early(other, 0, chunks)
            early(core, 0, chunks)
            b_to_c(0)

    for step in range(STEPS):
        beside(step)
        wait_halo(step)
        update_h(step, step == 0)
        if step < STEPS - 1:
            update_below(step, step == 0)
            update_e(step)
            stage(step + 1)
            send_halo(step + 1)
            sample(step)
        else:
            sample(step)
            last(other)
            begin_a(1)
            last(core)
            update_below(step, False)
            update_e(step)
    a_to_b(1)
    scale = float(tiles * members) ** (-0.5)
    old = end_c(0)
    for step in range(STEPS):
        end_halo(step)
    b_to_c(1)
    far_ref[...] = jnp.zeros_like(far_ref)
    new = end_c(1)
    used = min(new_rows, NB - hpast)
    for q in range(share // 128):
        columns = slice(q * 128, q * 128 + 128)
        far_ref[0:old_rows, columns] = old[q] * scale
        far_ref[hpast : hpast + used, columns] = (
            far_ref[hpast : hpast + used, columns] + (new[q] * scale)[0:used]
        )


def store_kernel(e_ref, far_ref, eout_ref, fout_ref, sem):
    bins = far_ref.shape[0]
    stores = [pltpu.make_async_copy(e_ref, eout_ref, sem.at[bins])] + [
        pltpu.make_async_copy(far_ref.at[b : b + 1], fout_ref.at[b], sem.at[b]) for b in range(bins)
    ]
    for store in stores:
        store.start()
    for store in stores:
        store.wait()


def up8(n):
    return (n + 7) // 8 * 8


def local(sizes, initial_field, inv_permittivity, history, tile_rows, owners, delays, weights):
    n_x, n_y, n_z = sizes
    sx, sy, sz = inv_permittivity.shape
    tiles, hpast, width = history.shape
    cap = max(2, 2 * tiles // n_x)
    slots = n_x * cap
    members = n_y * n_z
    plane_n = n_y * (n_z // 2)
    directions = weights.shape[1]
    share = directions // members
    old_rows, new_rows = up8(hpast + LAG - 1), up8(STEPS + LAG - 1)
    dims = (n_x, n_y, n_z, sx, sy, sz, tiles, hpast, cap, old_rows, new_rows, share)
    anywhere, resident = pl.BlockSpec(memory_space=pl.ANY), pl.BlockSpec(memory_space=pltpu.VMEM)
    f32, bf16 = jnp.float32, jnp.bfloat16
    vmem = pltpu.VMEM
    faces = lambda low: [
        vmem((STEPS, low, sy, sz), f32), vmem((STEPS, low, sx, sz), f32), vmem((STEPS, sy, sz), f32)
    ]
    flat, rows8 = vmem((STEPS, sy, sz), f32), vmem((STEPS, 8, sz), f32)
    edges = [flat, rows8] + [vmem((STEPS, 2, sx, sz), f32)] * 2 + [rows8, flat]
    below = [vmem((2, sy, sz), f32), vmem((2, sx, sz), f32), vmem((2, sy, sz), f32)]
    per_set = lambda make: [make(n_x * old_rows, old_rows), make(n_x * new_rows, new_rows)]
    scratch = (
        [vmem((3, sx, sy, sz), f32), vmem((sx, sy, sz), f32)]
        + [vmem((hpast, tiles, width), bf16), vmem((1, tiles), jnp.int32), vmem((1, tiles), jnp.int32)]
        + [vmem(delays.shape, jnp.int32), vmem(weights.shape, bf16)]
        + faces(2)
        + faces(3)
        + faces(2)
        + faces(3)
        + edges
        + below
        + [
            vmem((hpast * slots, width), bf16),
            vmem((STEPS * slots, width), bf16),
            vmem((slots, directions), f32),
            vmem((max(hpast, STEPS) * slots, WIDE), f32),
        ]
        + per_set(lambda rows, one: vmem((members, share // 128, rows, 128), f32))
        + per_set(lambda rows, one: vmem((plane_n, share // 128, rows, 128), f32))
        + per_set(lambda rows, one: vmem((plane_n, share // 128, rows, 128), f32))
        + per_set(lambda rows, one: vmem((plane_n, share // 128, rows, 128), f32))
        + per_set(lambda rows, one: vmem((share // 128, rows, 128), f32))
        + per_set(lambda rows, one: vmem((n_x, share // 128, one, 128), f32))
        + [pltpu.SemaphoreType.DMA((STEPS, 12))] * 2
        + [pltpu.SemaphoreType.DMA((2, plane_n))] * 2
        + [pltpu.SemaphoreType.DMA((3, plane_n))] * 2
        + [pltpu.SemaphoreType.DMA((2, n_x))] * 2
        + [pltpu.SemaphoreType.DMA((7,))]
    )
    efield, far = pl.pallas_call(
        functools.partial(kernel, dims),
        out_shape=(vmem(initial_field.shape, f32), vmem((NB, share), f32)),
        in_specs=[anywhere] * 7,
        out_specs=(resident, resident),
        scratch_shapes=scratch,
        compiler_params=pltpu.CompilerParams(
            collective_id=0, has_side_effects=True, vmem_limit_bytes=56 * 1024 * 1024
        ),
    )(
        initial_field, inv_permittivity, jnp.transpose(history, (1, 0, 2)),
        tile_rows[None], owners.reshape(1, tiles), delays, weights,
    )
    efield = pltpu.with_memory_space_constraint(efield, pltpu.VMEM)
    far = pltpu.with_memory_space_constraint(far, pltpu.VMEM)
    efield, far = pl.pallas_call(
        store_kernel,
        out_shape=(
            jax.ShapeDtypeStruct(initial_field.shape, f32), jax.ShapeDtypeStruct((NB, 1, share), f32)
        ),
        in_specs=[resident, resident],
        out_specs=(anywhere, anywhere),
        scratch_shapes=[pltpu.SemaphoreType.DMA((NB + 1,))],
    )(efield, far)
    return efield, jnp.transpose(far, (1, 0, 2))


def solution(mesh):
    placed = (
        P(None, "gx", "gy", "gz"),
        P("gx", "gy", "gz"),
        P(("gx", "gy", "gz"), None, None),
        P(("gx", "gy", "gz")),
        P(("gx", "gy", "gz"), None),
        P(("gx", "gy", "gz"), None),
        P(),
    )
    sizes = (mesh.shape["gx"], mesh.shape["gy"], mesh.shape["gz"])
    return jax.shard_map(
        functools.partial(local, sizes),
        mesh=mesh,
        in_specs=placed,
        out_specs=(P(None, "gx", "gy", "gz"), P("gx", None, ("gy", "gz"))),
        check_vma=False,
    )
```

```python
import functools

import jax
import jax.numpy as jnp
from jax import lax
from jax.experimental import pallas as pl
from jax.experimental.pallas import tpu as pltpu
from jax.sharding import PartitionSpec as P

STEPS = 4
LAG = 4
NB = 20

courant = 0.5
MESH = pl.DeviceIdType.MESH
WIDE = 256


def kernel(
    dims,
    field_ref, perm_ref, hist_hbm, rows_hbm, owners_hbm, delays_hbm, weights_hbm,
    e, far_ref,
    h, perm, hist_ref, rows_ref, owners_ref, delays_ref, weights_ref,
    xs, ys, zs, xt, yt, zt,
    xr, yr, zr, xl, yl, zl, exz, eyz, exy, ezy, eyx, ezx,
    hxm, hym, hzm,
    placed_past, placed_new, placed_delay, proj, proj_one,
    part_old, part_mid, part_new, recv_a_old, recv_a_mid, recv_a_new, sum_a_old, sum_a_mid, sum_a_new,
    recv_b_old, recv_b_mid, recv_b_new, sum_b_old, sum_b_mid, sum_b_new,
    out_c_old, out_c_mid, out_c_new, recv_c_old, recv_c_mid, recv_c_new,
    hs_sem, hr_sem, a_send, a_recv, b_send, b_recv, c_send, c_recv, in_sem,
):
    n_x, n_y, n_z, sx, sy, sz, tiles, hpast, cap, share = dims
    gx, gy, gz = lax.axis_index("gx"), lax.axis_index("gy"), lax.axis_index("gz")
    core, plane_z = gz % 2, gz // 2
    plane_n = n_y * (n_z // 2)
    plane_me = gy * (n_z // 2) + plane_z
    slots = n_x * cap
    wide_rows = max(8, n_x)
    groups = slots // wide_rows
    members = n_y * n_z

    loads = [
        pltpu.make_async_copy(source, target, in_sem.at[i])
        for i, (source, target) in enumerate(
            (
                (field_ref, e), (owners_hbm, owners_ref), (rows_hbm, rows_ref), (hist_hbm, hist_ref),
                (delays_hbm, delays_ref), (perm_ref, perm), (weights_hbm, weights_ref),
            )
        )
    ]
    for load in loads:
        load.start()

    for ref in (xr, yr, zr, xl, yl, zl, exz, eyz, exy, ezy, eyx, ezx, out_c_old, out_c_mid, out_c_new):
        ref[...] = jnp.zeros_like(ref)

    barrier = pltpu.get_barrier_semaphore()
    for j in range(1, n_x):
        pl.semaphore_signal(barrier, inc=1, device_id=((gx + j) % n_x, gy, gz), device_id_type=MESH)
    member_me = gy * n_z + gz
    for j in range(1, members):
        other = (member_me + j) % members
        pl.semaphore_signal(
            barrier, inc=1, device_id=(gx, other // n_z, other % n_z), device_id_type=MESH
        )

    tail = slice(sy - 8, sy)
    copies = (
        ((-1, 0, 0), lambda k: xs.at[k], lambda k: xr.at[k]),
        ((1, 0, 0), lambda k: xt.at[k], lambda k: xl.at[k]),
        ((1, 0, -1), lambda k: zs.at[k], lambda k: exz.at[k]),
        ((-1, 0, 1), lambda k: xs.at[k, 1], lambda k: ezx.at[k]),
        ((1, -1, 0), lambda k: ys.at[k], lambda k: exy.at[k]),
        ((-1, 1, 0), lambda k: xs.at[k, 0, tail], lambda k: eyx.at[k]),
        ((0, 1, -1), lambda k: zs.at[k, tail], lambda k: eyz.at[k]),
        ((0, -1, 1), lambda k: ys.at[k], lambda k: ezy.at[k]),
        ((0, -1, 0), lambda k: ys.at[k], lambda k: yr.at[k]),
        ((0, 1, 0), lambda k: yt.at[k], lambda k: yl.at[k]),
        ((0, 0, -1), lambda k: zs.at[k], lambda k: zr.at[k]),
        ((0, 0, 1), lambda k: zt.at[k], lambda k: zl.at[k]),
    )

    def at_offset(offset, sign):
        inside, place = None, []
        for pos, count, step in zip((gx, gy, gz), (n_x, n_y, n_z), offset):
            step = sign * step
            if step:
                fits = (pos > 0) if step < 0 else (pos < count - 1)
                inside = fits if inside is None else jnp.logical_and(inside, fits)
            place.append(jnp.clip(pos + step, 0, count - 1) if step else pos)
        return inside, tuple(place)

    diagonals = ((1, 0, -1), (-1, 0, 1), (1, -1, 0), (-1, 1, 0))
    for ox, oy, oz in diagonals:
        target = ((gx + ox + n_x) % n_x, (gy + oy + n_y) % n_y, (gz + oz + n_z) % n_z)
        pl.semaphore_signal(barrier, inc=1, device_id=target, device_id_type=MESH)

    lane = lax.broadcasted_iota(jnp.int32, (sy, sz), 1)
    row = lax.broadcasted_iota(jnp.int32, (sy, sz), 0)

    def stage(slot):
        for i, c in enumerate((1, 2)):
            xs[slot, i] = e[c, 0]
        for c in range(3):
            xt[slot, c] = e[c, sx - 1]
        for i, c in enumerate((0, 2)):
            for x in range(sx):
                ys[slot, i, x : x + 1, :] = e[c, x, 0:1, :]
        for c in range(3):
            for x in range(sx):
                yt[slot, c, x : x + 1, :] = e[c, x, sy - 1 : sy, :]
        low = jnp.zeros((sy, sz), jnp.float32)
        high = jnp.zeros((sy, sz), jnp.float32)
        for c in range(3):
            for x in range(sx):
                at = c * sx + x
                if c < 2:
                    low = jnp.where(lane == at, pltpu.roll(e[c, x], at, 1), low)
                high = jnp.where(lane == at, pltpu.roll(e[c, x], at + 1, 1), high)
        zs[slot] = low
        zt[slot] = high

    def halo_copy(slot, number):
        offset, source, target = copies[number]
        return pltpu.make_async_remote_copy(
            src_ref=source(slot), dst_ref=target(slot),
            send_sem=hs_sem.at[slot, number], recv_sem=hr_sem.at[slot, number],
            device_id=at_offset(offset, 1)[1], device_id_type=MESH,
        )

    def send_halo(slot):
        for number in range(len(copies)):
            @pl.when(at_offset(copies[number][0], 1)[0])
            def _():
                halo_copy(slot, number).start()

    def wait_halo(slot):
        for number in range(len(copies)):
            @pl.when(at_offset(copies[number][0], -1)[0])
            def _():
                halo_copy(slot, number).wait_recv()

    def end_halo(slot):
        for number in range(len(copies)):
            @pl.when(at_offset(copies[number][0], 1)[0])
            def _():
                halo_copy(slot, number).wait_send()

    def next_y(v, slot, i, x, low):
        if low:
            return jnp.where(row == 0, hym[i, x : x + 1, :], pltpu.roll(v, 1, 0))
        return jnp.where(row == sy - 1, yr[slot, i, x : x + 1, :], pltpu.roll(v, sy - 1, 0))

    def next_z(v, c, x, packed, low):
        if low:
            return jnp.where(
                lane == 0, pltpu.roll(hzm[c], (sz - x) % sz, 1), pltpu.roll(v, 1, 1)
            )
        at = c * sx + x
        return jnp.where(
            lane == sz - 1, pltpu.roll(packed, (sz - 1 - at) % sz, 1), pltpu.roll(v, sz - 1, 1)
        )

    def next_x(ref, slot, i, c, x, low):
        if low:
            return ref[c, x - 1] if x > 0 else hxm[i]
        return ref[c, x + 1] if x < sx - 1 else xr[slot, i]

    lane8 = lax.broadcasted_iota(jnp.int32, (sx, sz), 1)
    row8 = lax.broadcasted_iota(jnp.int32, (sx, sz), 0)

    def update_below(slot, first):
        def put(ref, i, change, exists):
            fresh = -change if first else ref[i] - change
            ref[i] = jnp.where(exists, fresh, 0.0)

        ex, ey, ez = xl[slot, 0], xl[slot, 1], xl[slot, 2]
        ex_z = jnp.where(
            lane == sz - 1, pltpu.roll(exz[slot], sz - sx, 1), pltpu.roll(ex, sz - 1, 1)
        )
        ex_y = jnp.where(row == sy - 1, exy[slot, 0, sx - 1 : sx, :], pltpu.roll(ex, sy - 1, 0))
        put(hxm, 0, courant * ((ex_z - ex) - (xs[slot, 1] - ez)), gx > 0)
        put(hxm, 1, courant * ((xs[slot, 0] - ey) - (ex_y - ex)), gx > 0)

        ex, ey, ez = yl[slot, 0], yl[slot, 1], yl[slot, 2]
        edge = jnp.sum(
            jnp.where(lane8 == row8 + sx, jnp.broadcast_to(eyz[slot, 7:8, :], (sx, sz)), 0.0),
            axis=1, keepdims=True,
        )
        ey_z = jnp.where(lane8 == sz - 1, edge, pltpu.roll(ey, sz - 1, 1))
        ey_x = jnp.where(row8 == sx - 1, eyx[slot, 7:8, :], pltpu.roll(ey, sx - 1, 0))
        put(hym, 0, courant * ((ys[slot, 1] - ez) - (ey_z - ey)), gy > 0)
        put(hym, 1, courant * ((ey_x - ey) - (ys[slot, 0] - ex)), gy > 0)

        ex = zl[slot]
        ey = pltpu.roll(ex, sz - sx, 1)
        ez = pltpu.roll(ex, sz - 2 * sx, 1)
        ex_up = zs[slot]
        ey_up = pltpu.roll(ex_up, sz - sx, 1)
        column = jnp.sum(jnp.where(lane8 == sz - 1, ezy[slot, 1], 0.0), axis=1, keepdims=True)
        edge = jnp.sum(jnp.where(lane8 == row8, column, 0.0), axis=0, keepdims=True)
        ez_y = jnp.where(row == sy - 1, edge, pltpu.roll(ez, sy - 1, 0))
        ez_x = jnp.where(lane == sx - 1, pltpu.roll(ezx[slot], sx, 1), pltpu.roll(ez, sz - 1, 1))
        put(hzm, 0, courant * ((ez_y - ez) - (ey_up - ey)), gz > 0)
        put(hzm, 1, courant * ((ex_up - ex) - (ez_x - ez)), gz > 0)

    def update_h(slot, first):
        packed = zr[slot]
        for x in range(sx):
            ex, ey, ez = e[0, x], e[1, x], e[2, x]
            ez_y, ex_y = next_y(ez, slot, 1, x, False), next_y(ex, slot, 0, x, False)
            ey_z, ex_z = next_z(ey, 1, x, packed, False), next_z(ex, 0, x, packed, False)
            ez_x, ey_x = next_x(e, slot, 1, 2, x, False), next_x(e, slot, 0, 1, x, False)
            changes = (
                courant * ((ez_y - ez) - (ey_z - ey)),
                courant * ((ex_z - ex) - (ez_x - ez)),
                courant * ((ey_x - ey) - (ex_y - ex)),
            )
            for c in range(3):
                h[c, x] = -changes[c] if first else h[c, x] - changes[c]

    def update_e(slot):
        for x in range(sx):
            hx, hy, hz = h[0, x], h[1, x], h[2, x]
            hz_y, hx_y = next_y(hz, slot, 1, x, True), next_y(hx, slot, 0, x, True)
            hy_z, hx_z = next_z(hy, 1, x, None, True), next_z(hx, 0, x, None, True)
            hz_x, hy_x = next_x(h, slot, 1, 2, x, True), next_x(h, slot, 0, 1, x, True)
            scale = courant * perm[x]
            e[0, x] = e[0, x] + scale * ((hz - hz_y) - (hy - hy_z))
            e[1, x] = e[1, x] + scale * ((hx - hx_z) - (hz - hz_x))
            e[2, x] = e[2, x] + scale * ((hy - hy_x) - (hx - hx_y))

    loads[0].wait()
    stage(0)

    loads[1].wait()
    loads[2].wait()
    owner_row = owners_ref[...]
    ti = lax.broadcasted_iota(jnp.int32, (tiles, tiles), 0)
    tj = lax.broadcasted_iota(jnp.int32, (tiles, tiles), 1)
    owner_wide = jnp.broadcast_to(owner_row, (tiles, tiles))
    owner_col = jnp.sum(jnp.where(ti == tj, owner_wide, 0), axis=1, keepdims=True)
    rank_row = jnp.sum(
        jnp.where((owner_col == owner_wide) & (ti < tj), 1, 0), axis=0, keepdims=True
    )
    slot_row = rank_row * n_x + owner_row
    slot_ids = lax.broadcasted_iota(jnp.int32, (slots, tiles), 0)
    place = jnp.where(slot_ids == slot_row, 1.0, 0.0).astype(jnp.bfloat16)
    pick = jnp.where(
        lax.broadcasted_iota(jnp.int32, (sx * sy, tiles), 0) == rows_ref[...], 1.0, 0.0
    ).astype(jnp.bfloat16)
    sampler = lax.dot_general(
        place, pick, (((1,), (1,)), ((), ())), preferred_element_type=jnp.float32
    ).astype(jnp.bfloat16)

    pl.semaphore_wait(barrier, n_x - 1 + members - 1 + len(diagonals))
    send_halo(0)

    loads[3].wait()
    for t in range(hpast):
        placed_past[t * slots : (t + 1) * slots, :] = jnp.dot(
            place, hist_ref[t], preferred_element_type=jnp.float32
        ).astype(jnp.bfloat16)
    loads[4].wait()
    placed_delay[...] = jnp.dot(
        place, delays_ref[...].astype(jnp.float32).astype(jnp.bfloat16),
        preferred_element_type=jnp.float32,
    )
    loads[5].wait()
    loads[6].wait()

    low_half = lax.broadcasted_iota(jnp.int32, (8, 128), 0) < 4
    zero = jnp.zeros((8, 128), jnp.float32)

    def shift_add(held, buf, times, base, column, piece, block, total):
        for g in range(groups):
            spot = g * wide_rows + block * 8
            late = placed_delay[spot : spot + 8, pl.ds(column, 128)]
            far_late = late > 1.5
            odd = jnp.where(far_late, late - 2.0, late) > 0.5
            value, once = None, [None, None]
            for b in range(times + LAG - 1):
                before, value = value, None
                if b < times:
                    at = b * slots + spot
                    value = held[buf, at : at + 8, piece * 128 : piece * 128 + 128]
                one = None
                if value is not None or before is not None:
                    one = jnp.where(odd, zero if before is None else before, zero if value is None else value)
                two = once[0]
                once = [once[1], one]
                moved = jnp.where(far_late, zero if two is None else two, zero if one is None else one)
                total[base + b] = moved if total[base + b] is None else total[base + b] + moved

    def keep(part, member, inside, block, total, add):
        def put(first, value):
            spot = slice(first, first + value.shape[0])
            if add:
                value = part[member, inside, spot, :] + value
            part[member, inside, spot, :] = value

        if n_x == 4:
            for b in range(0, len(total), 2):
                pair = total[b : b + 2]
                if add and all(v is None for v in pair):
                    continue
                first, second = [zero if v is None else v for v in pair]
                across = jnp.where(low_half, second, first)
                put(b * n_x, jnp.where(low_half, first, second) + pltpu.roll(across, 4, 0))
            return
        for b, value in enumerate(total):
            if value is None:
                if add:
                    continue
                value = zero
            if n_x < 8:
                whole = value
                value = whole[0:n_x]
                for other in range(n_x, 8, n_x):
                    value = value + whole[other : other + n_x]
            put(b * n_x + block * 8, value)

    def project(source, time0, times, base, which, add, parity, held, wide):
        part = sets[which][0]
        bins = part.shape[2] // n_x
        per = share // wide
        count = plane_n * per

        def multiply(i, buf):
            member = 2 * (i // per) + parity
            start = pl.multiple_of(member * share + (i % per) * wide, wide)
            held[buf, 0 : times * slots, :] = jnp.dot(
                source[time0 * slots : (time0 + times) * slots, :], weights_ref[:, pl.ds(start, wide)],
                preferred_element_type=jnp.float32,
            )

        def gather(i, buf):
            member = 2 * (i // per) + parity
            for q in range(wide // 128):
                inside = (i % per) * (wide // 128) + q
                column = pl.multiple_of(member * share + inside * 128, 128)
                for block in range(wide_rows // 8):
                    total = [None] * bins
                    shift_add(held, buf, times, base, column, q, block, total)
                    keep(part, member, inside, block, total, add)

        def body(k, carry):
            multiply(2 * k + 1, 1)
            gather(2 * k, 0)
            multiply(2 * k + 2, 0)
            gather(2 * k + 1, 1)
            return carry

        multiply(0, 0)
        lax.fori_loop(0, count // 2 - 1, body, 0)
        multiply(count - 1, 1)
        gather(count - 2, 0)
        gather(count - 1, 1)

    sets = (
        (part_old, recv_a_old, sum_a_old, recv_b_old, sum_b_old, out_c_old, recv_c_old),
        (part_mid, recv_a_mid, sum_a_mid, recv_b_mid, sum_b_mid, out_c_mid, recv_c_mid),
        (part_new, recv_a_new, sum_a_new, recv_b_new, sum_b_new, out_c_new, recv_c_new),
    )
    kept_bins = (hpast + LAG - 1, STEPS - 1 + LAG - 1, LAG)

    def copy_a(which, m):
        part, recv = sets[which][0], sets[which][1]
        other = 1 - core
        return pltpu.make_async_remote_copy(
            src_ref=part.at[2 * m + other], dst_ref=recv.at[m],
            send_sem=a_send.at[which, m], recv_sem=a_recv.at[which, m],
            device_id=(gx, gy, plane_z * 2 + other), device_id_type=MESH,
        )

    blocks = share // 128
    cuts = ((0, blocks // 2, blocks), (0, blocks), (0, blocks))
    b_base = (0, 2, 3)

    def copy_b(which, piece, j):
        span = slice(cuts[which][piece], cuts[which][piece + 1])
        summed, recv = sets[which][2], sets[which][3]
        other = (plane_me + j) % plane_n
        half = n_z // 2
        return pltpu.make_async_remote_copy(
            src_ref=summed.at[other, span], dst_ref=recv.at[j, span],
            send_sem=b_send.at[b_base[which] + piece, j], recv_sem=b_recv.at[b_base[which] + piece, j],
            device_id=(gx, other // half, (other % half) * 2 + core), device_id_type=MESH,
        )

    def copy_c(which, j):
        source, recv = sets[which][5], sets[which][6]
        other = (gx + j) % n_x
        return pltpu.make_async_remote_copy(
            src_ref=source.at[other], dst_ref=recv.at[j],
            send_sem=c_send.at[which, j], recv_sem=c_recv.at[which, j],
            device_id=(other, gy, gz), device_id_type=MESH,
        )

    def begin_a(which):
        for m in range(plane_n):
            copy_a(which, m).start()

    def a_to_b(which):
        part, recv, summed = sets[which][0], sets[which][1], sets[which][2]
        for j in list(range(1, plane_n)) + [0]:
            m = (plane_me + j) % plane_n
            copy_a(which, m).wait_recv()
            summed[m] = part[2 * m + core] + recv[m]
            if j > 0:
                copy_b(which, 0, j).start()

    def b_to_c(which):
        total = sets[which][2][plane_me]
        for j in range(1, plane_n):
            for piece in range(len(cuts[which]) - 1):
                copy_b(which, piece, j).wait_recv()
            total = total + sets[which][3][j]
        summed, source = sets[which][4], sets[which][5]
        summed[...] = total
        many = kept_bins[which]
        for s in range(n_x):
            for q in range(blocks):
                source[s, q, 0:many, :] = summed[q, pl.ds(s, many, stride=n_x), :]
        for j in range(1, n_x):
            copy_c(which, j).start()

    def end_c(which):
        total = sets[which][5][gx]
        for j in range(1, n_x):
            copy_c(which, j).wait_recv()
            total = total + sets[which][6][j]
        for m in range(plane_n):
            copy_a(which, m).wait_send()
        for j in range(1, plane_n):
            for piece in range(len(cuts[which]) - 1):
                copy_b(which, piece, j).wait_send()
        for j in range(1, n_x):
            copy_c(which, j).wait_send()
        return total

    other = 1 - core

    def sample(step):
        for m in range(2):
            flat = h[m].reshape(sx * sy, sz).astype(jnp.bfloat16)
            placed_new[step * slots : (step + 1) * slots, m * sz : (m + 1) * sz] = jnp.dot(
                sampler, flat, preferred_element_type=jnp.float32
            ).astype(jnp.bfloat16)

    def past(parity):
        project(placed_past, 0, hpast, 0, 0, False, parity, proj, WIDE)

    def recent(parity, step):
        if step < STEPS - 1:
            project(placed_new, step, 1, step, 1, step > 0, parity, proj_one, share)
        else:
            project(placed_new, step, 1, 0, 2, False, parity, proj_one, share)

    def beside(step):
        if step == 0:
            past(other)
            begin_a(0)
            past(core)
        elif step == 1:
            a_to_b(0)
            recent(other, 0)
            recent(core, 0)
        elif step == 2:
            for j in range(1, plane_n):
                copy_b(0, 1, j).start()
            recent(other, 1)
            recent(core, 1)
        elif step == 3:
            recent(other, 2)
            begin_a(1)
            recent(core, 2)
            a_to_b(1)
            b_to_c(0)

    for step in range(STEPS):
        beside(step)
        wait_halo(step)
        update_h(step, step == 0)
        if step < STEPS - 1:
            update_below(step, step == 0)
            update_e(step)
            stage(step + 1)
            send_halo(step + 1)
            sample(step)
        else:
            sample(step)
            recent(other, step)
            begin_a(2)
            recent(core, step)
            a_to_b(2)
            update_below(step, False)
            update_e(step)
    scale = float(tiles * members) ** (-0.5)
    for step in range(STEPS):
        end_halo(step)
    b_to_c(1)
    old = end_c(0)
    far_ref[...] = jnp.zeros_like(far_ref)
    for q in range(blocks):
        far_ref[0 : kept_bins[0], q * 128 : q * 128 + 128] = (old[q] * scale)[0 : kept_bins[0]]
    b_to_c(2)
    for which, first in ((1, hpast), (2, hpast + STEPS - 1)):
        many = kept_bins[which]
        total = end_c(which)
        for q in range(blocks):
            columns = slice(q * 128, q * 128 + 128)
            far_ref[first : first + many, columns] = (
                far_ref[first : first + many, columns] + (total[q] * scale)[0:many]
            )


def store_kernel(e_ref, far_ref, eout_ref, fout_ref, sem):
    bins = far_ref.shape[0]
    stores = [pltpu.make_async_copy(e_ref, eout_ref, sem.at[bins])] + [
        pltpu.make_async_copy(far_ref.at[b : b + 1], fout_ref.at[b], sem.at[b]) for b in range(bins)
    ]
    for store in stores:
        store.start()
    for store in stores:
        store.wait()


def up8(n):
    return (n + 7) // 8 * 8


def local(sizes, initial_field, inv_permittivity, history, tile_rows, owners, delays, weights):
    n_x, n_y, n_z = sizes
    sx, sy, sz = inv_permittivity.shape
    tiles, hpast, width = history.shape
    cap = max(2, 2 * tiles // n_x)
    slots = n_x * cap
    members = n_y * n_z
    plane_n = n_y * (n_z // 2)
    directions = weights.shape[1]
    share = directions // members
    dims = (n_x, n_y, n_z, sx, sy, sz, tiles, hpast, cap, share)
    kept_bins = (hpast + LAG - 1, STEPS - 1 + LAG - 1, LAG)
    anywhere, resident = pl.BlockSpec(memory_space=pl.ANY), pl.BlockSpec(memory_space=pltpu.VMEM)
    f32, bf16 = jnp.float32, jnp.bfloat16
    vmem = pltpu.VMEM
    faces = lambda low: [
        vmem((STEPS, low, sy, sz), f32), vmem((STEPS, low, sx, sz), f32), vmem((STEPS, sy, sz), f32)
    ]
    flat, rows8 = vmem((STEPS, sy, sz), f32), vmem((STEPS, 8, sz), f32)
    edges = [flat, rows8] + [vmem((STEPS, 2, sx, sz), f32)] * 2 + [rows8, flat]
    below = [vmem((2, sy, sz), f32), vmem((2, sx, sz), f32), vmem((2, sy, sz), f32)]
    per_set = lambda make: [make(up8(n_x * bins), up8(bins)) for bins in kept_bins]
    scratch = (
        [vmem((3, sx, sy, sz), f32), vmem((sx, sy, sz), f32)]
        + [vmem((hpast, tiles, width), bf16), vmem((1, tiles), jnp.int32), vmem((1, tiles), jnp.int32)]
        + [vmem(delays.shape, jnp.int32), vmem(weights.shape, bf16)]
        + faces(2)
        + faces(3)
        + faces(2)
        + faces(3)
        + edges
        + below
        + [
            vmem((hpast * slots, width), bf16),
            vmem((STEPS * slots, width), bf16),
            vmem((slots, directions), f32),
            vmem((2, hpast * slots, WIDE), f32),
            vmem((2, slots, share), f32),
        ]
        + per_set(lambda rows, one: vmem((members, share // 128, rows, 128), f32))
        + per_set(lambda rows, one: vmem((plane_n, share // 128, rows, 128), f32))
        + per_set(lambda rows, one: vmem((plane_n, share // 128, rows, 128), f32))
        + per_set(lambda rows, one: vmem((plane_n, share // 128, rows, 128), f32))
        + per_set(lambda rows, one: vmem((share // 128, rows, 128), f32))
        + per_set(lambda rows, one: vmem((n_x, share // 128, one, 128), f32))
        + per_set(lambda rows, one: vmem((n_x, share // 128, one, 128), f32))
        + [pltpu.SemaphoreType.DMA((STEPS, 12))] * 2
        + [pltpu.SemaphoreType.DMA((3, plane_n))] * 2
        + [pltpu.SemaphoreType.DMA((4, plane_n))] * 2
        + [pltpu.SemaphoreType.DMA((3, n_x))] * 2
        + [pltpu.SemaphoreType.DMA((7,))]
    )
    efield, far = pl.pallas_call(
        functools.partial(kernel, dims),
        out_shape=(vmem(initial_field.shape, f32), vmem((NB, share), f32)),
        in_specs=[anywhere] * 7,
        out_specs=(resident, resident),
        scratch_shapes=scratch,
        compiler_params=pltpu.CompilerParams(
            collective_id=0, has_side_effects=True, vmem_limit_bytes=56 * 1024 * 1024
        ),
    )(
        initial_field, inv_permittivity, jnp.transpose(history, (1, 0, 2)),
        tile_rows[None], owners.reshape(1, tiles), delays, weights,
    )
    efield = pltpu.with_memory_space_constraint(efield, pltpu.VMEM)
    far = pltpu.with_memory_space_constraint(far, pltpu.VMEM)
    efield, far = pl.pallas_call(
        store_kernel,
        out_shape=(
            jax.ShapeDtypeStruct(initial_field.shape, f32), jax.ShapeDtypeStruct((NB, 1, share), f32)
        ),
        in_specs=[resident, resident],
        out_specs=(anywhere, anywhere),
        scratch_shapes=[pltpu.SemaphoreType.DMA((NB + 1,))],
    )(efield, far)
    return efield, jnp.transpose(far, (1, 0, 2))


def solution(mesh):
    placed = (
        P(None, "gx", "gy", "gz"),
        P("gx", "gy", "gz"),
        P(("gx", "gy", "gz"), None, None),
        P(("gx", "gy", "gz")),
        P(("gx", "gy", "gz"), None),
        P(("gx", "gy", "gz"), None),
        P(),
    )
    sizes = (mesh.shape["gx"], mesh.shape["gy"], mesh.shape["gz"])
    return jax.shard_map(
        functools.partial(local, sizes),
        mesh=mesh,
        in_specs=placed,
        out_specs=(P(None, "gx", "gy", "gz"), P("gx", None, ("gy", "gz"))),
        check_vma=False,
    )
```

```python
import functools

import jax
import jax.numpy as jnp
from jax import lax
from jax.experimental import pallas as pl
from jax.experimental.pallas import tpu as pltpu
from jax.sharding import PartitionSpec as P

STEPS = 4
LAG = 4
NB = 20

courant = 0.5
MESH = pl.DeviceIdType.MESH


def kernel(
    dims,
    field_ref, perm_ref, hist_hbm, rows_hbm, owners_hbm, delays_hbm, weights_hbm,
    e, far_ref,
    h, perm, hist_ref, rows_ref, owners_ref, delays_ref, weights_ref,
    xs, ys, zs, xt, yt, zt, cx, cz,
    xr, yr, zr, xl, yl, zl, exz, eyz, exy, ezy, eyx, ezx,
    hxm, hym, hzm,
    placed_past, placed_new, placed_delay, proj, proj_one,
    part_old, part_mid, part_new, recv_a_old, recv_a_mid, recv_a_new, sum_a_old, sum_a_mid, sum_a_new,
    recv_b_old, recv_b_mid, recv_b_new, sum_b_old, sum_b_mid, sum_b_new,
    out_c_old, out_c_mid, out_c_new, recv_c_old, recv_c_mid, recv_c_new,
    hs_sem, hr_sem, a_send, a_recv, b_send, b_recv, c_send, c_recv, in_sem,
):
    n_x, n_y, n_z, sx, sy, sz, tiles, hpast, cap, share = dims
    gx, gy, gz = lax.axis_index("gx"), lax.axis_index("gy"), lax.axis_index("gz")
    core, plane_z = gz % 2, gz // 2
    plane_n = n_y * (n_z // 2)
    plane_me = gy * (n_z // 2) + plane_z
    slots = n_x * cap
    wide_rows = max(8, n_x)
    groups = slots // wide_rows
    members = n_y * n_z

    loads = [
        pltpu.make_async_copy(source, target, in_sem.at[i])
        for i, (source, target) in enumerate(
            (
                (field_ref, e), (owners_hbm, owners_ref), (rows_hbm, rows_ref), (hist_hbm, hist_ref),
                (delays_hbm, delays_ref), (perm_ref, perm), (weights_hbm, weights_ref),
            )
        )
    ]
    for load in loads:
        load.start()

    for ref in (xr, yr, zr, xl, yl, zl, exz, eyz, exy, ezy, eyx, ezx, out_c_old, out_c_mid, out_c_new):
        ref[...] = jnp.zeros_like(ref)

    barrier = pltpu.get_barrier_semaphore()
    for j in range(1, n_x):
        pl.semaphore_signal(barrier, inc=1, device_id=((gx + j) % n_x, gy, gz), device_id_type=MESH)
    member_me = gy * n_z + gz
    for j in range(1, members):
        other = (member_me + j) % members
        pl.semaphore_signal(
            barrier, inc=1, device_id=(gx, other // n_z, other % n_z), device_id_type=MESH
        )

    tail = slice(sy - 8, sy)
    copies = (
        ((1, 0, -1), lambda k: cz.at[k], lambda k: exz.at[k]),
        ((-1, 0, 1), lambda k: cx.at[k], lambda k: ezx.at[k]),
        ((1, -1, 0), lambda k: ys.at[k, 0], lambda k: exy.at[k]),
        ((-1, 1, 0), lambda k: xs.at[k, 0, tail], lambda k: eyx.at[k]),
        ((1, 0, 0), lambda k: xt.at[k], lambda k: xl.at[k]),
        ((-1, 0, 0), lambda k: xs.at[k], lambda k: xr.at[k]),
        ((0, 1, -1), lambda k: zs.at[k, tail], lambda k: eyz.at[k]),
        ((0, -1, 1), lambda k: ys.at[k, 1], lambda k: ezy.at[k]),
        ((0, -1, 0), lambda k: ys.at[k], lambda k: yr.at[k]),
        ((0, 1, 0), lambda k: yt.at[k], lambda k: yl.at[k]),
        ((0, 0, -1), lambda k: zs.at[k], lambda k: zr.at[k]),
        ((0, 0, 1), lambda k: zt.at[k], lambda k: zl.at[k]),
    )

    def at_offset(offset, sign):
        inside, place = None, []
        for pos, count, step in zip((gx, gy, gz), (n_x, n_y, n_z), offset):
            step = sign * step
            if step:
                fits = (pos > 0) if step < 0 else (pos < count - 1)
                inside = fits if inside is None else jnp.logical_and(inside, fits)
            place.append(jnp.clip(pos + step, 0, count - 1) if step else pos)
        return inside, tuple(place)

    diagonals = ((1, 0, -1), (-1, 0, 1), (1, -1, 0), (-1, 1, 0))
    for ox, oy, oz in diagonals:
        target = ((gx + ox + n_x) % n_x, (gy + oy + n_y) % n_y, (gz + oz + n_z) % n_z)
        pl.semaphore_signal(barrier, inc=1, device_id=target, device_id_type=MESH)

    lane = lax.broadcasted_iota(jnp.int32, (sy, sz), 1)
    row = lax.broadcasted_iota(jnp.int32, (sy, sz), 0)

    lane_row = lax.broadcasted_iota(jnp.int32, (8, sz), 1)

    def pack_column(v, at):
        tile = jnp.zeros((8, sz), jnp.float32)
        for j in range(sy // 8):
            tile = jnp.where(lane_row == j, pltpu.roll(v[8 * j : 8 * j + 8], (j - at) % sz, 1), tile)
        return tile

    def spread_column(tile, at):
        return jnp.concatenate([pltpu.roll(tile, (at - j) % sz, 1) for j in range(sy // 8)], axis=0)

    def stage(slot):
        for i, c in enumerate((1, 2)):
            xs[slot, i] = e[c, 0]
        ex, ey, ez = e[0, sx - 1], e[1, sx - 1], e[2, sx - 1]
        ex_z = jnp.where(lane == sz - 1, 0.0, pltpu.roll(ex, sz - 1, 1))
        ex_y = jnp.where(row == sy - 1, 0.0, pltpu.roll(ex, sy - 1, 0))
        xt[slot, 0] = (ex_z - ex) + ez
        xt[slot, 1] = (ex - ex_y) - ey
        cz[slot] = pack_column(ex, 0)
        cx[slot] = pack_column(e[2, 0], sz - 1)
        for i, c in enumerate((0, 2)):
            for x in range(sx):
                ys[slot, i, x : x + 1, :] = e[c, x, 0:1, :]
        for c in range(3):
            for x in range(sx):
                yt[slot, c, x : x + 1, :] = e[c, x, sy - 1 : sy, :]
        low = jnp.zeros((sy, sz), jnp.float32)
        high = jnp.zeros((sy, sz), jnp.float32)
        for c in range(3):
            for x in range(sx):
                at = c * sx + x
                if c < 2:
                    low = jnp.where(lane == at, pltpu.roll(e[c, x], at, 1), low)
                high = jnp.where(lane == at, pltpu.roll(e[c, x], at + 1, 1), high)
        zs[slot] = low
        zt[slot] = high

    def halo_copy(slot, number):
        offset, source, target = copies[number]
        return pltpu.make_async_remote_copy(
            src_ref=source(slot), dst_ref=target(slot),
            send_sem=hs_sem.at[slot, number], recv_sem=hr_sem.at[slot, number],
            device_id=at_offset(offset, 1)[1], device_id_type=MESH,
        )

    def send_halo(slot):
        for number in range(len(copies)):
            @pl.when(at_offset(copies[number][0], 1)[0])
            def _():
                halo_copy(slot, number).start()

    def wait_halo(slot):
        for number in range(len(copies)):
            @pl.when(at_offset(copies[number][0], -1)[0])
            def _():
                halo_copy(slot, number).wait_recv()

    def end_halo(slot):
        for number in range(len(copies)):
            @pl.when(at_offset(copies[number][0], 1)[0])
            def _():
                halo_copy(slot, number).wait_send()

    def next_y(v, slot, i, x, low):
        if low:
            return jnp.where(row == 0, hym[i, x : x + 1, :], pltpu.roll(v, 1, 0))
        return jnp.where(row == sy - 1, yr[slot, i, x : x + 1, :], pltpu.roll(v, sy - 1, 0))

    def next_z(v, c, x, packed, low):
        if low:
            return jnp.where(
                lane == 0, pltpu.roll(hzm[c], (sz - x) % sz, 1), pltpu.roll(v, 1, 1)
            )
        at = c * sx + x
        return jnp.where(
            lane == sz - 1, pltpu.roll(packed, (sz - 1 - at) % sz, 1), pltpu.roll(v, sz - 1, 1)
        )

    def next_x(ref, slot, i, c, x, low):
        if low:
            return ref[c, x - 1] if x > 0 else hxm[i]
        return ref[c, x + 1] if x < sx - 1 else xr[slot, i]

    lane8 = lax.broadcasted_iota(jnp.int32, (sx, sz), 1)
    row8 = lax.broadcasted_iota(jnp.int32, (sx, sz), 0)

    def update_below(slot, first):
        def put(ref, i, change, exists):
            fresh = -change if first else ref[i] - change
            ref[i] = jnp.where(exists, fresh, 0.0)

        ex_z = jnp.where(lane == sz - 1, spread_column(exz[slot], sz - 1), 0.0)
        ex_y = jnp.where(row == sy - 1, exy[slot, sx - 1 : sx, :], 0.0)
        put(hxm, 0, courant * ((xl[slot, 0] + ex_z) - xs[slot, 1]), gx > 0)
        put(hxm, 1, courant * ((xl[slot, 1] - ex_y) + xs[slot, 0]), gx > 0)

        ex, ey, ez = yl[slot, 0], yl[slot, 1], yl[slot, 2]
        edge = jnp.sum(
            jnp.where(lane8 == row8 + sx, jnp.broadcast_to(eyz[slot, 7:8, :], (sx, sz)), 0.0),
            axis=1, keepdims=True,
        )
        ey_z = jnp.where(lane8 == sz - 1, edge, pltpu.roll(ey, sz - 1, 1))
        ey_x = jnp.where(row8 == sx - 1, eyx[slot, 7:8, :], pltpu.roll(ey, sx - 1, 0))
        put(hym, 0, courant * ((ys[slot, 1] - ez) - (ey_z - ey)), gy > 0)
        put(hym, 1, courant * ((ey_x - ey) - (ys[slot, 0] - ex)), gy > 0)

        ex = zl[slot]
        ey = pltpu.roll(ex, sz - sx, 1)
        ez = pltpu.roll(ex, sz - 2 * sx, 1)
        ex_up = zs[slot]
        ey_up = pltpu.roll(ex_up, sz - sx, 1)
        column = jnp.sum(jnp.where(lane8 == sz - 1, ezy[slot], 0.0), axis=1, keepdims=True)
        edge = jnp.sum(jnp.where(lane8 == row8, column, 0.0), axis=0, keepdims=True)
        ez_y = jnp.where(row == sy - 1, edge, pltpu.roll(ez, sy - 1, 0))
        ez_x = jnp.where(lane == sx - 1, spread_column(ezx[slot], sx - 1), pltpu.roll(ez, sz - 1, 1))
        put(hzm, 0, courant * ((ez_y - ez) - (ey_up - ey)), gz > 0)
        put(hzm, 1, courant * ((ex_up - ex) - (ez_x - ez)), gz > 0)

    def update_h(slot, first):
        packed = zr[slot]
        for x in range(sx):
            ex, ey, ez = e[0, x], e[1, x], e[2, x]
            ez_y, ex_y = next_y(ez, slot, 1, x, False), next_y(ex, slot, 0, x, False)
            ey_z, ex_z = next_z(ey, 1, x, packed, False), next_z(ex, 0, x, packed, False)
            ez_x, ey_x = next_x(e, slot, 1, 2, x, False), next_x(e, slot, 0, 1, x, False)
            changes = (
                courant * ((ez_y - ez) - (ey_z - ey)),
                courant * ((ex_z - ex) - (ez_x - ez)),
                courant * ((ey_x - ey) - (ex_y - ex)),
            )
            for c in range(3):
                h[c, x] = -changes[c] if first else h[c, x] - changes[c]

    def update_e(slot):
        for x in range(sx):
            hx, hy, hz = h[0, x], h[1, x], h[2, x]
            hz_y, hx_y = next_y(hz, slot, 1, x, True), next_y(hx, slot, 0, x, True)
            hy_z, hx_z = next_z(hy, 1, x, None, True), next_z(hx, 0, x, None, True)
            hz_x, hy_x = next_x(h, slot, 1, 2, x, True), next_x(h, slot, 0, 1, x, True)
            scale = courant * perm[x]
            e[0, x] = e[0, x] + scale * ((hz - hz_y) - (hy - hy_z))
            e[1, x] = e[1, x] + scale * ((hx - hx_z) - (hz - hz_x))
            e[2, x] = e[2, x] + scale * ((hy - hy_x) - (hx - hx_y))

    loads[0].wait()
    stage(0)

    loads[1].wait()
    loads[2].wait()
    owner_row = owners_ref[...]
    ti = lax.broadcasted_iota(jnp.int32, (tiles, tiles), 0)
    tj = lax.broadcasted_iota(jnp.int32, (tiles, tiles), 1)
    owner_wide = jnp.broadcast_to(owner_row, (tiles, tiles))
    owner_col = jnp.sum(jnp.where(ti == tj, owner_wide, 0), axis=1, keepdims=True)
    rank_row = jnp.sum(
        jnp.where((owner_col == owner_wide) & (ti < tj), 1, 0), axis=0, keepdims=True
    )
    slot_row = rank_row * n_x + owner_row
    slot_ids = lax.broadcasted_iota(jnp.int32, (slots, tiles), 0)
    place = jnp.where(slot_ids == slot_row, 1.0, 0.0).astype(jnp.bfloat16)
    pick = jnp.where(
        lax.broadcasted_iota(jnp.int32, (sx * sy, tiles), 0) == rows_ref[...], 1.0, 0.0
    ).astype(jnp.bfloat16)
    sampler = lax.dot_general(
        place, pick, (((1,), (1,)), ((), ())), preferred_element_type=jnp.float32
    ).astype(jnp.bfloat16)

    pl.semaphore_wait(barrier, n_x - 1 + members - 1 + len(diagonals))
    send_halo(0)

    loads[3].wait()
    for t in range(hpast):
        placed_past[t * slots : (t + 1) * slots, :] = jnp.dot(
            place, hist_ref[t], preferred_element_type=jnp.float32
        ).astype(jnp.bfloat16)
    loads[4].wait()
    placed_delay[...] = jnp.dot(
        place, delays_ref[...].astype(jnp.float32).astype(jnp.bfloat16),
        preferred_element_type=jnp.float32,
    )
    loads[5].wait()
    loads[6].wait()

    low_half = lax.broadcasted_iota(jnp.int32, (8, 128), 0) < 4
    zero = jnp.zeros((8, 128), jnp.float32)

    def shift_add(held, buf, times, base, column, piece, block, total):
        for g in range(groups):
            spot = g * wide_rows + block * 8
            late = placed_delay[spot : spot + 8, pl.ds(column, 128)]
            far_late = late > 1.5
            odd = jnp.where(far_late, late - 2.0, late) > 0.5
            value, once = None, [None, None]
            for b in range(times + LAG - 1):
                before, value = value, None
                if b < times:
                    at = b * slots + spot
                    value = held[buf, at : at + 8, piece * 128 : piece * 128 + 128]
                one = None
                if value is not None or before is not None:
                    one = jnp.where(odd, zero if before is None else before, zero if value is None else value)
                two = once[0]
                once = [once[1], one]
                moved = jnp.where(far_late, zero if two is None else two, zero if one is None else one)
                total[base + b] = moved if total[base + b] is None else total[base + b] + moved

    def keep(part, member, inside, block, total, add):
        def put(first, value):
            spot = slice(first, first + value.shape[0])
            if add:
                value = part[member, inside, spot, :] + value
            part[member, inside, spot, :] = value

        if n_x == 4:
            for b in range(0, len(total), 2):
                pair = total[b : b + 2]
                if add and all(v is None for v in pair):
                    continue
                first, second = [zero if v is None else v for v in pair]
                across = jnp.where(low_half, second, first)
                put(b * n_x, jnp.where(low_half, first, second) + pltpu.roll(across, 4, 0))
            return
        for b, value in enumerate(total):
            if value is None:
                if add:
                    continue
                value = zero
            if n_x < 8:
                whole = value
                value = whole[0:n_x]
                for other in range(n_x, 8, n_x):
                    value = value + whole[other : other + n_x]
            put(b * n_x + block * 8, value)

    def project(source, time0, times, base, which, add, parity, held, wide, half):
        part = sets[which][0]
        bins = part.shape[2] // n_x

        def multiply(m, buf):
            start = pl.multiple_of((2 * m + parity) * share + half * wide, 128)
            held[buf, 0 : times * slots, :] = jnp.dot(
                source[time0 * slots : (time0 + times) * slots, :], weights_ref[:, pl.ds(start, wide)],
                preferred_element_type=jnp.float32,
            )

        def gather(m, buf):
            member = 2 * m + parity
            for q in range(wide // 128):
                inside = half * (wide // 128) + q
                column = pl.multiple_of(member * share + inside * 128, 128)
                for block in range(wide_rows // 8):
                    total = [None] * bins
                    shift_add(held, buf, times, base, column, q, block, total)
                    keep(part, member, inside, block, total, add)

        def body(k, carry):
            multiply(2 * k + 1, 1)
            gather(2 * k, 0)
            multiply(2 * k + 2, 0)
            gather(2 * k + 1, 1)
            return carry

        multiply(0, 0)
        lax.fori_loop(0, plane_n // 2 - 1, body, 0)
        multiply(plane_n - 1, 1)
        gather(plane_n - 2, 0)
        gather(plane_n - 1, 1)

    sets = (
        (part_old, recv_a_old, sum_a_old, recv_b_old, sum_b_old, out_c_old, recv_c_old),
        (part_mid, recv_a_mid, sum_a_mid, recv_b_mid, sum_b_mid, out_c_mid, recv_c_mid),
        (part_new, recv_a_new, sum_a_new, recv_b_new, sum_b_new, out_c_new, recv_c_new),
    )
    kept_bins = (hpast + LAG - 1, STEPS - 1 + LAG - 1, LAG)

    blocks = share // 128
    cuts = ((0, blocks // 2, blocks), (0, blocks), (0, blocks))
    sem_base = (0, 2, 3)

    def copy_a(which, piece, m):
        span = slice(cuts[which][piece], cuts[which][piece + 1])
        part, recv = sets[which][0], sets[which][1]
        other = 1 - core
        return pltpu.make_async_remote_copy(
            src_ref=part.at[2 * m + other, span], dst_ref=recv.at[m, span],
            send_sem=a_send.at[sem_base[which] + piece, m], recv_sem=a_recv.at[sem_base[which] + piece, m],
            device_id=(gx, gy, plane_z * 2 + other), device_id_type=MESH,
        )

    def copy_b(which, piece, j):
        span = slice(cuts[which][piece], cuts[which][piece + 1])
        summed, recv = sets[which][2], sets[which][3]
        other = (plane_me + j) % plane_n
        half = n_z // 2
        return pltpu.make_async_remote_copy(
            src_ref=summed.at[other, span], dst_ref=recv.at[j, span],
            send_sem=b_send.at[sem_base[which] + piece, j], recv_sem=b_recv.at[sem_base[which] + piece, j],
            device_id=(gx, other // half, (other % half) * 2 + core), device_id_type=MESH,
        )

    def copy_c(which, j):
        source, recv = sets[which][5], sets[which][6]
        other = (gx + j) % n_x
        return pltpu.make_async_remote_copy(
            src_ref=source.at[other], dst_ref=recv.at[j],
            send_sem=c_send.at[which, j], recv_sem=c_recv.at[which, j],
            device_id=(other, gy, gz), device_id_type=MESH,
        )

    def begin_a(which, piece):
        for m in range(plane_n):
            copy_a(which, piece, m).start()

    def a_to_b(which, piece):
        span = slice(cuts[which][piece], cuts[which][piece + 1])
        part, recv, summed = sets[which][0], sets[which][1], sets[which][2]
        for j in list(range(1, plane_n)) + [0]:
            m = (plane_me + j) % plane_n
            copy_a(which, piece, m).wait_recv()
            summed[m, span] = part[2 * m + core, span] + recv[m, span]
            if j > 0:
                copy_b(which, piece, j).start()

    def b_to_c(which):
        total = sets[which][2][plane_me]
        for j in range(1, plane_n):
            for piece in range(len(cuts[which]) - 1):
                copy_b(which, piece, j).wait_recv()
            total = total + sets[which][3][j]
        summed, source = sets[which][4], sets[which][5]
        summed[...] = total
        many = kept_bins[which]
        for s in range(n_x):
            for q in range(blocks):
                source[s, q, 0:many, :] = summed[q, pl.ds(s, many, stride=n_x), :]
        for j in range(1, n_x):
            copy_c(which, j).start()

    def end_c(which):
        total = sets[which][5][gx]
        for j in range(1, n_x):
            copy_c(which, j).wait_recv()
            total = total + sets[which][6][j]
        for m in range(plane_n):
            for piece in range(len(cuts[which]) - 1):
                copy_a(which, piece, m).wait_send()
        for j in range(1, plane_n):
            for piece in range(len(cuts[which]) - 1):
                copy_b(which, piece, j).wait_send()
        for j in range(1, n_x):
            copy_c(which, j).wait_send()
        return total

    other = 1 - core

    def sample(step):
        for m in range(2):
            flat = h[m].reshape(sx * sy, sz).astype(jnp.bfloat16)
            placed_new[step * slots : (step + 1) * slots, m * sz : (m + 1) * sz] = jnp.dot(
                sampler, flat, preferred_element_type=jnp.float32
            ).astype(jnp.bfloat16)

    def past(half):
        for parity in (other, core):
            project(placed_past, 0, hpast, 0, 0, False, parity, proj, share // 2, half)
            if parity is other:
                begin_a(0, half)

    def recent(step):
        which = 1 if step < STEPS - 1 else 2
        base = step if step < STEPS - 1 else 0
        for parity in (other, core):
            project(placed_new, step, 1, base, which, 0 < step < STEPS - 1, parity, proj_one, share, 0)
            if parity is other and step >= STEPS - 2:
                begin_a(which, 0)

    def beside(step):
        if step == 0:
            past(0)
        elif step == 1:
            a_to_b(0, 0)
            past(1)
            recent(0)
        elif step == 2:
            a_to_b(0, 1)
            recent(1)
        elif step == 3:
            recent(2)
            b_to_c(0)
            a_to_b(1, 0)

    for step in range(STEPS):
        beside(step)
        wait_halo(step)
        update_h(step, step == 0)
        if step < STEPS - 1:
            update_below(step, step == 0)
            update_e(step)
            stage(step + 1)
            send_halo(step + 1)
            sample(step)
        else:
            sample(step)
            recent(step)
            a_to_b(2, 0)
            update_below(step, False)
            update_e(step)
    scale = float(tiles * members) ** (-0.5)
    for step in range(STEPS):
        end_halo(step)
    b_to_c(1)
    old = end_c(0)
    far_ref[...] = jnp.zeros_like(far_ref)
    for q in range(blocks):
        far_ref[0 : kept_bins[0], q * 128 : q * 128 + 128] = (old[q] * scale)[0 : kept_bins[0]]
    b_to_c(2)
    for which, first in ((1, hpast), (2, hpast + STEPS - 1)):
        many = kept_bins[which]
        total = end_c(which)
        for q in range(blocks):
            columns = slice(q * 128, q * 128 + 128)
            far_ref[first : first + many, columns] = (
                far_ref[first : first + many, columns] + (total[q] * scale)[0:many]
            )


def store_kernel(e_ref, far_ref, eout_ref, fout_ref, sem):
    bins = far_ref.shape[0]
    stores = [pltpu.make_async_copy(e_ref, eout_ref, sem.at[bins])] + [
        pltpu.make_async_copy(far_ref.at[b : b + 1], fout_ref.at[b], sem.at[b]) for b in range(bins)
    ]
    for store in stores:
        store.start()
    for store in stores:
        store.wait()


def up8(n):
    return (n + 7) // 8 * 8


def local(sizes, initial_field, inv_permittivity, history, tile_rows, owners, delays, weights):
    n_x, n_y, n_z = sizes
    sx, sy, sz = inv_permittivity.shape
    tiles, hpast, width = history.shape
    cap = max(2, 2 * tiles // n_x)
    slots = n_x * cap
    members = n_y * n_z
    plane_n = n_y * (n_z // 2)
    directions = weights.shape[1]
    share = directions // members
    dims = (n_x, n_y, n_z, sx, sy, sz, tiles, hpast, cap, share)
    kept_bins = (hpast + LAG - 1, STEPS - 1 + LAG - 1, LAG)
    anywhere, resident = pl.BlockSpec(memory_space=pl.ANY), pl.BlockSpec(memory_space=pltpu.VMEM)
    f32, bf16 = jnp.float32, jnp.bfloat16
    vmem = pltpu.VMEM
    faces = lambda in_x, in_y: [
        vmem((STEPS, in_x, sy, sz), f32), vmem((STEPS, in_y, sx, sz), f32), vmem((STEPS, sy, sz), f32)
    ]
    rows8 = vmem((STEPS, 8, sz), f32)
    edges = [rows8, rows8] + [vmem((STEPS, sx, sz), f32)] * 2 + [rows8, rows8]
    below = [vmem((2, sy, sz), f32), vmem((2, sx, sz), f32), vmem((2, sy, sz), f32)]
    per_set = lambda make: [make(up8(n_x * bins), up8(bins)) for bins in kept_bins]
    scratch = (
        [vmem((3, sx, sy, sz), f32), vmem((sx, sy, sz), f32)]
        + [vmem((hpast, tiles, width), bf16), vmem((1, tiles), jnp.int32), vmem((1, tiles), jnp.int32)]
        + [vmem(delays.shape, jnp.int32), vmem(weights.shape, bf16)]
        + faces(2, 2)
        + faces(2, 3)
        + [rows8, rows8]
        + faces(2, 2)
        + faces(2, 3)
        + edges
        + below
        + [
            vmem((hpast * slots, width), bf16),
            vmem((STEPS * slots, width), bf16),
            vmem((slots, directions), f32),
            vmem((2, hpast * slots, share // 2), f32),
            vmem((2, slots, share), f32),
        ]
        + per_set(lambda rows, one: vmem((members, share // 128, rows, 128), f32))
        + per_set(lambda rows, one: vmem((plane_n, share // 128, rows, 128), f32))
        + per_set(lambda rows, one: vmem((plane_n, share // 128, rows, 128), f32))
        + per_set(lambda rows, one: vmem((plane_n, share // 128, rows, 128), f32))
        + per_set(lambda rows, one: vmem((share // 128, rows, 128), f32))
        + per_set(lambda rows, one: vmem((n_x, share // 128, one, 128), f32))
        + per_set(lambda rows, one: vmem((n_x, share // 128, one, 128), f32))
        + [pltpu.SemaphoreType.DMA((STEPS, 12))] * 2
        + [pltpu.SemaphoreType.DMA((4, plane_n))] * 4
        + [pltpu.SemaphoreType.DMA((3, n_x))] * 2
        + [pltpu.SemaphoreType.DMA((7,))]
    )
    efield, far = pl.pallas_call(
        functools.partial(kernel, dims),
        out_shape=(vmem(initial_field.shape, f32), vmem((NB, share), f32)),
        in_specs=[anywhere] * 7,
        out_specs=(resident, resident),
        scratch_shapes=scratch,
        compiler_params=pltpu.CompilerParams(
            collective_id=0, has_side_effects=True, vmem_limit_bytes=56 * 1024 * 1024
        ),
    )(
        initial_field, inv_permittivity, jnp.transpose(history, (1, 0, 2)),
        tile_rows[None], owners.reshape(1, tiles), delays, weights,
    )
    efield = pltpu.with_memory_space_constraint(efield, pltpu.VMEM)
    far = pltpu.with_memory_space_constraint(far, pltpu.VMEM)
    efield, far = pl.pallas_call(
        store_kernel,
        out_shape=(
            jax.ShapeDtypeStruct(initial_field.shape, f32), jax.ShapeDtypeStruct((NB, 1, share), f32)
        ),
        in_specs=[resident, resident],
        out_specs=(anywhere, anywhere),
        scratch_shapes=[pltpu.SemaphoreType.DMA((NB + 1,))],
    )(efield, far)
    return efield, jnp.transpose(far, (1, 0, 2))


def solution(mesh):
    placed = (
        P(None, "gx", "gy", "gz"),
        P("gx", "gy", "gz"),
        P(("gx", "gy", "gz"), None, None),
        P(("gx", "gy", "gz")),
        P(("gx", "gy", "gz"), None),
        P(("gx", "gy", "gz"), None),
        P(),
    )
    sizes = (mesh.shape["gx"], mesh.shape["gy"], mesh.shape["gz"])
    return jax.shard_map(
        functools.partial(local, sizes),
        mesh=mesh,
        in_specs=placed,
        out_specs=(P(None, "gx", "gy", "gz"), P("gx", None, ("gy", "gz"))),
        check_vma=False,
    )
```

```python
import functools

import jax
import jax.numpy as jnp
from jax import lax
from jax.experimental import pallas as pl
from jax.experimental.pallas import tpu as pltpu
from jax.sharding import PartitionSpec as P

STEPS = 4
LAG = 4
NB = 20

courant = 0.5
MESH = pl.DeviceIdType.MESH


def kernel(
    dims,
    field_ref, perm_ref, hist_hbm, rows_hbm, owners_hbm, delays_hbm, weights_hbm,
    e, far_ref,
    h, perm, hist_ref, rows_ref, owners_ref, delays_ref, weights_ref,
    xs, ys, zs, xt, yt, zt, cx, cz,
    xr, yr, zr, xl, yl, zl, exz, eyz, exy, ezy, eyx, ezx,
    hxm, hym, hzm,
    placed_past, placed_new, placed_delay, proj, proj_one,
    part_old, part_mid, part_new, recv_a_old, recv_a_mid, recv_a_new, sum_a_old, sum_a_mid, sum_a_new,
    recv_b_old, recv_b_mid, recv_b_new, sum_b_old, sum_b_mid, sum_b_new,
    out_c_old, out_c_mid, out_c_new, recv_c_old, recv_c_mid, recv_c_new,
    hs_sem, hr_sem, a_send, a_recv, b_send, b_recv, c_send, c_recv, in_sem,
):
    n_x, n_y, n_z, sx, sy, sz, tiles, hpast, cap, share = dims
    gx, gy, gz = lax.axis_index("gx"), lax.axis_index("gy"), lax.axis_index("gz")
    core, plane_z = gz % 2, gz // 2
    plane_n = n_y * (n_z // 2)
    plane_me = gy * (n_z // 2) + plane_z
    slots = n_x * cap
    wide_rows = max(8, n_x)
    groups = slots // wide_rows
    members = n_y * n_z

    loads = [
        pltpu.make_async_copy(source, target, in_sem.at[i])
        for i, (source, target) in enumerate(
            (
                (field_ref, e), (owners_hbm, owners_ref), (rows_hbm, rows_ref), (hist_hbm, hist_ref),
                (delays_hbm, delays_ref), (perm_ref, perm), (weights_hbm, weights_ref),
            )
        )
    ]
    for load in loads:
        load.start()

    for ref in (xr, yr, zr, xl, yl, zl, exz, eyz, exy, ezy, eyx, ezx, out_c_old, out_c_mid, out_c_new):
        ref[...] = jnp.zeros_like(ref)

    barrier = pltpu.get_barrier_semaphore()
    for j in range(1, n_x):
        pl.semaphore_signal(barrier, inc=1, device_id=((gx + j) % n_x, gy, gz), device_id_type=MESH)
    member_me = gy * n_z + gz
    for j in range(1, members):
        other = (member_me + j) % members
        pl.semaphore_signal(
            barrier, inc=1, device_id=(gx, other // n_z, other % n_z), device_id_type=MESH
        )

    tail = slice(sy - 8, sy)
    copies = (
        ((1, 0, -1), lambda k: cz.at[k], lambda k: exz.at[k]),
        ((-1, 0, 1), lambda k: cx.at[k], lambda k: ezx.at[k]),
        ((1, -1, 0), lambda k: ys.at[k, 0], lambda k: exy.at[k]),
        ((-1, 1, 0), lambda k: xs.at[k, 0, tail], lambda k: eyx.at[k]),
        ((1, 0, 0), lambda k: xt.at[k], lambda k: xl.at[k]),
        ((-1, 0, 0), lambda k: xs.at[k], lambda k: xr.at[k]),
        ((0, 1, -1), lambda k: zs.at[k, tail], lambda k: eyz.at[k]),
        ((0, -1, 1), lambda k: ys.at[k, 1], lambda k: ezy.at[k]),
        ((0, -1, 0), lambda k: ys.at[k], lambda k: yr.at[k]),
        ((0, 1, 0), lambda k: yt.at[k], lambda k: yl.at[k]),
        ((0, 0, -1), lambda k: zs.at[k], lambda k: zr.at[k]),
        ((0, 0, 1), lambda k: zt.at[k], lambda k: zl.at[k]),
    )

    def at_offset(offset, sign):
        inside, place = None, []
        for pos, count, step in zip((gx, gy, gz), (n_x, n_y, n_z), offset):
            step = sign * step
            if step:
                fits = (pos > 0) if step < 0 else (pos < count - 1)
                inside = fits if inside is None else jnp.logical_and(inside, fits)
            place.append(jnp.clip(pos + step, 0, count - 1) if step else pos)
        return inside, tuple(place)

    diagonals = ((1, 0, -1), (-1, 0, 1), (1, -1, 0), (-1, 1, 0))
    for ox, oy, oz in diagonals:
        target = ((gx + ox + n_x) % n_x, (gy + oy + n_y) % n_y, (gz + oz + n_z) % n_z)
        pl.semaphore_signal(barrier, inc=1, device_id=target, device_id_type=MESH)

    lane = lax.broadcasted_iota(jnp.int32, (sy, sz), 1)
    row = lax.broadcasted_iota(jnp.int32, (sy, sz), 0)

    lane_row = lax.broadcasted_iota(jnp.int32, (8, sz), 1)

    def pack_column(v, at):
        tile = jnp.zeros((8, sz), jnp.float32)
        for j in range(sy // 8):
            tile = jnp.where(lane_row == j, pltpu.roll(v[8 * j : 8 * j + 8], (j - at) % sz, 1), tile)
        return tile

    def spread_column(tile, at):
        return jnp.concatenate([pltpu.roll(tile, (at - j) % sz, 1) for j in range(sy // 8)], axis=0)

    def stage(slot):
        for i, c in enumerate((1, 2)):
            xs[slot, i] = e[c, 0]
        ex, ey, ez = e[0, sx - 1], e[1, sx - 1], e[2, sx - 1]
        ex_z = jnp.where(lane == sz - 1, 0.0, pltpu.roll(ex, sz - 1, 1))
        ex_y = jnp.where(row == sy - 1, 0.0, pltpu.roll(ex, sy - 1, 0))
        xt[slot, 0] = (ex_z - ex) + ez
        xt[slot, 1] = (ex - ex_y) - ey
        cz[slot] = pack_column(ex, 0)
        cx[slot] = pack_column(e[2, 0], sz - 1)
        for i, c in enumerate((0, 2)):
            for x in range(sx):
                ys[slot, i, x : x + 1, :] = e[c, x, 0:1, :]
        for c in range(3):
            for x in range(sx):
                yt[slot, c, x : x + 1, :] = e[c, x, sy - 1 : sy, :]
        low = jnp.zeros((sy, sz), jnp.float32)
        high = jnp.zeros((sy, sz), jnp.float32)
        for c in range(3):
            for x in range(sx):
                at = c * sx + x
                if c < 2:
                    low = jnp.where(lane == at, pltpu.roll(e[c, x], at, 1), low)
                high = jnp.where(lane == at, pltpu.roll(e[c, x], at + 1, 1), high)
        zs[slot] = low
        zt[slot] = high

    def halo_copy(slot, number):
        offset, source, target = copies[number]
        return pltpu.make_async_remote_copy(
            src_ref=source(slot), dst_ref=target(slot),
            send_sem=hs_sem.at[number], recv_sem=hr_sem.at[slot % 2, number],
            device_id=at_offset(offset, 1)[1], device_id_type=MESH,
        )

    def send_halo(slot):
        for number in range(len(copies)):
            @pl.when(at_offset(copies[number][0], 1)[0])
            def _():
                halo_copy(slot, number).start()

    def wait_halo(slot):
        for number in range(len(copies)):
            @pl.when(at_offset(copies[number][0], -1)[0])
            def _():
                halo_copy(slot, number).wait_recv()

    def end_halo(slot):
        for number in range(len(copies)):
            @pl.when(at_offset(copies[number][0], 1)[0])
            def _():
                halo_copy(slot, number).wait_send()

    def next_y(v, slot, i, x, low):
        if low:
            return jnp.where(row == 0, hym[i, x : x + 1, :], pltpu.roll(v, 1, 0))
        return jnp.where(row == sy - 1, yr[slot, i, x : x + 1, :], pltpu.roll(v, sy - 1, 0))

    def next_z(v, c, x, packed, low):
        if low:
            return jnp.where(
                lane == 0, pltpu.roll(hzm[c], (sz - x) % sz, 1), pltpu.roll(v, 1, 1)
            )
        at = c * sx + x
        return jnp.where(
            lane == sz - 1, pltpu.roll(packed, (sz - 1 - at) % sz, 1), pltpu.roll(v, sz - 1, 1)
        )

    def next_x(ref, slot, i, c, x, low):
        if low:
            return ref[c, x - 1] if x > 0 else hxm[i]
        return ref[c, x + 1] if x < sx - 1 else xr[slot, i]

    lane8 = lax.broadcasted_iota(jnp.int32, (sx, sz), 1)
    row8 = lax.broadcasted_iota(jnp.int32, (sx, sz), 0)

    def update_below(slot, first):
        def put(ref, i, change, exists):
            fresh = -change if first else ref[i] - change
            ref[i] = jnp.where(exists, fresh, 0.0)

        ex_z = jnp.where(lane == sz - 1, spread_column(exz[slot], sz - 1), 0.0)
        ex_y = jnp.where(row == sy - 1, exy[slot, sx - 1 : sx, :], 0.0)
        put(hxm, 0, courant * ((xl[slot, 0] + ex_z) - xs[slot, 1]), gx > 0)
        put(hxm, 1, courant * ((xl[slot, 1] - ex_y) + xs[slot, 0]), gx > 0)

        ex, ey, ez = yl[slot, 0], yl[slot, 1], yl[slot, 2]
        edge = jnp.sum(
            jnp.where(lane8 == row8 + sx, jnp.broadcast_to(eyz[slot, 7:8, :], (sx, sz)), 0.0),
            axis=1, keepdims=True,
        )
        ey_z = jnp.where(lane8 == sz - 1, edge, pltpu.roll(ey, sz - 1, 1))
        ey_x = jnp.where(row8 == sx - 1, eyx[slot, 7:8, :], pltpu.roll(ey, sx - 1, 0))
        put(hym, 0, courant * ((ys[slot, 1] - ez) - (ey_z - ey)), gy > 0)
        put(hym, 1, courant * ((ey_x - ey) - (ys[slot, 0] - ex)), gy > 0)

        ex = zl[slot]
        ey = pltpu.roll(ex, sz - sx, 1)
        ez = pltpu.roll(ex, sz - 2 * sx, 1)
        ex_up = zs[slot]
        ey_up = pltpu.roll(ex_up, sz - sx, 1)
        column = jnp.sum(jnp.where(lane8 == sz - 1, ezy[slot], 0.0), axis=1, keepdims=True)
        edge = jnp.sum(jnp.where(lane8 == row8, column, 0.0), axis=0, keepdims=True)
        ez_y = jnp.where(row == sy - 1, edge, pltpu.roll(ez, sy - 1, 0))
        ez_x = jnp.where(lane == sx - 1, spread_column(ezx[slot], sx - 1), pltpu.roll(ez, sz - 1, 1))
        put(hzm, 0, courant * ((ez_y - ez) - (ey_up - ey)), gz > 0)
        put(hzm, 1, courant * ((ex_up - ex) - (ez_x - ez)), gz > 0)

    def update_h(slot, first):
        packed = zr[slot]
        for x in range(sx):
            ex, ey, ez = e[0, x], e[1, x], e[2, x]
            ez_y, ex_y = next_y(ez, slot, 1, x, False), next_y(ex, slot, 0, x, False)
            ey_z, ex_z = next_z(ey, 1, x, packed, False), next_z(ex, 0, x, packed, False)
            ez_x, ey_x = next_x(e, slot, 1, 2, x, False), next_x(e, slot, 0, 1, x, False)
            changes = (
                courant * ((ez_y - ez) - (ey_z - ey)),
                courant * ((ex_z - ex) - (ez_x - ez)),
                courant * ((ey_x - ey) - (ex_y - ex)),
            )
            for c in range(3):
                h[c, x] = -changes[c] if first else h[c, x] - changes[c]

    def update_e(slot):
        for x in range(sx):
            hx, hy, hz = h[0, x], h[1, x], h[2, x]
            hz_y, hx_y = next_y(hz, slot, 1, x, True), next_y(hx, slot, 0, x, True)
            hy_z, hx_z = next_z(hy, 1, x, None, True), next_z(hx, 0, x, None, True)
            hz_x, hy_x = next_x(h, slot, 1, 2, x, True), next_x(h, slot, 0, 1, x, True)
            scale = courant * perm[x]
            e[0, x] = e[0, x] + scale * ((hz - hz_y) - (hy - hy_z))
            e[1, x] = e[1, x] + scale * ((hx - hx_z) - (hz - hz_x))
            e[2, x] = e[2, x] + scale * ((hy - hy_x) - (hx - hx_y))

    loads[0].wait()
    stage(0)

    loads[1].wait()
    loads[2].wait()
    owner_row = owners_ref[...]
    ti = lax.broadcasted_iota(jnp.int32, (tiles, tiles), 0)
    tj = lax.broadcasted_iota(jnp.int32, (tiles, tiles), 1)
    owner_wide = jnp.broadcast_to(owner_row, (tiles, tiles))
    owner_col = jnp.sum(jnp.where(ti == tj, owner_wide, 0), axis=1, keepdims=True)
    rank_row = jnp.sum(
        jnp.where((owner_col == owner_wide) & (ti < tj), 1, 0), axis=0, keepdims=True
    )
    slot_row = rank_row * n_x + owner_row
    slot_ids = lax.broadcasted_iota(jnp.int32, (slots, tiles), 0)
    place = jnp.where(slot_ids == slot_row, 1.0, 0.0).astype(jnp.bfloat16)
    pick = jnp.where(
        lax.broadcasted_iota(jnp.int32, (sx * sy, tiles), 0) == rows_ref[...], 1.0, 0.0
    ).astype(jnp.bfloat16)
    sampler = lax.dot_general(
        place, pick, (((1,), (1,)), ((), ())), preferred_element_type=jnp.float32
    ).astype(jnp.bfloat16)

    pl.semaphore_wait(barrier, n_x - 1 + members - 1 + len(diagonals))
    send_halo(0)

    loads[3].wait()
    for t in range(hpast):
        placed_past[t * slots : (t + 1) * slots, :] = jnp.dot(
            place, hist_ref[t], preferred_element_type=jnp.float32
        ).astype(jnp.bfloat16)
    loads[4].wait()
    placed_delay[...] = jnp.dot(
        place, delays_ref[...].astype(jnp.float32).astype(jnp.bfloat16),
        preferred_element_type=jnp.float32,
    )
    loads[5].wait()
    loads[6].wait()

    low_half = lax.broadcasted_iota(jnp.int32, (8, 128), 0) < 4
    zero = jnp.zeros((8, 128), jnp.float32)

    def shift_add(held, buf, times, base, column, piece, block, total):
        for g in range(groups):
            spot = g * wide_rows + block * 8
            late = placed_delay[spot : spot + 8, pl.ds(column, 128)]
            far_late = late > 1.5
            odd = jnp.where(far_late, late - 2.0, late) > 0.5
            value, once = None, [None, None]
            for b in range(times + LAG - 1):
                before, value = value, None
                if b < times:
                    at = b * slots + spot
                    value = held[buf, at : at + 8, piece * 128 : piece * 128 + 128]
                one = None
                if value is not None or before is not None:
                    one = jnp.where(odd, zero if before is None else before, zero if value is None else value)
                two = once[0]
                once = [once[1], one]
                moved = jnp.where(far_late, zero if two is None else two, zero if one is None else one)
                total[base + b] = moved if total[base + b] is None else total[base + b] + moved

    def keep(part, member, inside, block, total, add):
        def put(first, value):
            spot = slice(first, first + value.shape[0])
            if add:
                value = part[member, inside, spot, :] + value
            part[member, inside, spot, :] = value

        if n_x == 4:
            for b in range(0, len(total), 2):
                pair = total[b : b + 2]
                if add and all(v is None for v in pair):
                    continue
                first, second = [zero if v is None else v for v in pair]
                across = jnp.where(low_half, second, first)
                put(b * n_x, jnp.where(low_half, first, second) + pltpu.roll(across, 4, 0))
            return
        for b, value in enumerate(total):
            if value is None:
                if add:
                    continue
                value = zero
            if n_x < 8:
                whole = value
                value = whole[0:n_x]
                for other in range(n_x, 8, n_x):
                    value = value + whole[other : other + n_x]
            put(b * n_x + block * 8, value)

    def project(source, time0, times, base, which, add, parity, held, wide, half):
        part = sets[which][0]
        bins = part.shape[2] // n_x

        def multiply(m, buf):
            start = pl.multiple_of((2 * m + parity) * share + half * wide, 128)
            held[buf, 0 : times * slots, :] = jnp.dot(
                source[time0 * slots : (time0 + times) * slots, :], weights_ref[:, pl.ds(start, wide)],
                preferred_element_type=jnp.float32,
            )

        def gather(m, buf):
            member = 2 * m + parity
            for q in range(wide // 128):
                inside = half * (wide // 128) + q
                column = pl.multiple_of(member * share + inside * 128, 128)
                for block in range(wide_rows // 8):
                    total = [None] * bins
                    shift_add(held, buf, times, base, column, q, block, total)
                    keep(part, member, inside, block, total, add)

        def body(k, carry):
            multiply(2 * k + 1, 1)
            gather(2 * k, 0)
            multiply(2 * k + 2, 0)
            gather(2 * k + 1, 1)
            return carry

        multiply(0, 0)
        lax.fori_loop(0, plane_n // 2 - 1, body, 0)
        multiply(plane_n - 1, 1)
        gather(plane_n - 2, 0)
        gather(plane_n - 1, 1)

    sets = (
        (part_old, recv_a_old, sum_a_old, recv_b_old, sum_b_old, out_c_old, recv_c_old),
        (part_mid, recv_a_mid, sum_a_mid, recv_b_mid, sum_b_mid, out_c_mid, recv_c_mid),
        (part_new, recv_a_new, sum_a_new, recv_b_new, sum_b_new, out_c_new, recv_c_new),
    )
    kept_bins = (hpast + LAG - 1, STEPS - 1 + LAG - 1, LAG)

    blocks = share // 128
    cuts = ((0, blocks // 2, blocks), (0, blocks), (0, blocks))
    sem_base = (0, 2, 3)

    def copy_a(which, piece, m):
        span = slice(cuts[which][piece], cuts[which][piece + 1])
        part, recv = sets[which][0], sets[which][1]
        other = 1 - core
        return pltpu.make_async_remote_copy(
            src_ref=part.at[2 * m + other, span], dst_ref=recv.at[m, span],
            send_sem=a_send.at[m], recv_sem=a_recv.at[(sem_base[which] + piece) % 2, m],
            device_id=(gx, gy, plane_z * 2 + other), device_id_type=MESH,
        )

    def copy_b(which, piece, j):
        span = slice(cuts[which][piece], cuts[which][piece + 1])
        summed, recv = sets[which][2], sets[which][3]
        other = (plane_me + j) % plane_n
        half = n_z // 2
        return pltpu.make_async_remote_copy(
            src_ref=summed.at[other, span], dst_ref=recv.at[j, span],
            send_sem=b_send.at[j - 1], recv_sem=b_recv.at[sem_base[which] + piece, j - 1],
            device_id=(gx, other // half, (other % half) * 2 + core), device_id_type=MESH,
        )

    def copy_c(which, j):
        source, recv = sets[which][5], sets[which][6]
        other = (gx + j) % n_x
        return pltpu.make_async_remote_copy(
            src_ref=source.at[other], dst_ref=recv.at[j],
            send_sem=c_send.at[j - 1], recv_sem=c_recv.at[which, j - 1],
            device_id=(other, gy, gz), device_id_type=MESH,
        )

    turns = ((0, 0), (0, 1), (1, 0), (2, 0))

    def turn_before(which, piece):
        at = turns.index((which, piece))
        return turns[at - 1] if at > 0 else None

    def begin_a(which, piece):
        before = turn_before(which, piece)
        for m in range(plane_n):
            if before:
                copy_a(*before, m).wait_send()
            copy_a(which, piece, m).start()

    def a_to_b(which, piece):
        span = slice(cuts[which][piece], cuts[which][piece + 1])
        part, recv, summed = sets[which][0], sets[which][1], sets[which][2]
        for j in list(range(1, plane_n)) + [0]:
            m = (plane_me + j) % plane_n
            copy_a(which, piece, m).wait_recv()
            summed[m, span] = part[2 * m + core, span] + recv[m, span]
            if j > 0:
                if turn_before(which, piece):
                    copy_b(*turn_before(which, piece), j).wait_send()
                copy_b(which, piece, j).start()

    def b_to_c(which):
        total = sets[which][2][plane_me]
        for j in range(1, plane_n):
            for piece in range(len(cuts[which]) - 1):
                copy_b(which, piece, j).wait_recv()
            total = total + sets[which][3][j]
        summed, source = sets[which][4], sets[which][5]
        summed[...] = total
        many = kept_bins[which]
        for s in range(n_x):
            for q in range(blocks):
                source[s, q, 0:many, :] = summed[q, pl.ds(s, many, stride=n_x), :]
        for j in range(1, n_x):
            if which > 0:
                copy_c(which - 1, j).wait_send()
            copy_c(which, j).start()

    def end_c(which):
        total = sets[which][5][gx]
        for j in range(1, n_x):
            copy_c(which, j).wait_recv()
            total = total + sets[which][6][j]
        if which == 2:
            for m in range(plane_n):
                copy_a(which, 0, m).wait_send()
            for j in range(1, plane_n):
                copy_b(which, 0, j).wait_send()
            for j in range(1, n_x):
                copy_c(which, j).wait_send()
        return total

    other = 1 - core

    def sample(step):
        for m in range(2):
            flat = h[m].reshape(sx * sy, sz).astype(jnp.bfloat16)
            placed_new[step * slots : (step + 1) * slots, m * sz : (m + 1) * sz] = jnp.dot(
                sampler, flat, preferred_element_type=jnp.float32
            ).astype(jnp.bfloat16)

    def past(half):
        for parity in (other, core):
            project(placed_past, 0, hpast, 0, 0, False, parity, proj, share // 2, half)
            if parity is other:
                begin_a(0, half)

    def recent(step):
        which = 1 if step < STEPS - 1 else 2
        base = step if step < STEPS - 1 else 0
        for parity in (other, core):
            project(placed_new, step, 1, base, which, 0 < step < STEPS - 1, parity, proj_one, share, 0)
            if parity is other and step >= STEPS - 2:
                begin_a(which, 0)

    def beside(step):
        if step == 0:
            past(0)
        elif step == 1:
            a_to_b(0, 0)
            past(1)
            recent(0)
        elif step == 2:
            a_to_b(0, 1)
            recent(1)
        elif step == 3:
            recent(2)
            b_to_c(0)
            a_to_b(1, 0)

    for step in range(STEPS):
        beside(step)
        wait_halo(step)
        update_h(step, step == 0)
        if step < STEPS - 1:
            update_below(step, step == 0)
            update_e(step)
            stage(step + 1)
            end_halo(step)
            send_halo(step + 1)
            sample(step)
        else:
            sample(step)
            recent(step)
            a_to_b(2, 0)
            update_below(step, False)
            update_e(step)
    scale = float(tiles * members) ** (-0.5)
    end_halo(STEPS - 1)
    b_to_c(1)
    old = end_c(0)
    far_ref[...] = jnp.zeros_like(far_ref)
    for q in range(blocks):
        far_ref[0 : kept_bins[0], q * 128 : q * 128 + 128] = (old[q] * scale)[0 : kept_bins[0]]
    b_to_c(2)
    for which, first in ((1, hpast), (2, hpast + STEPS - 1)):
        many = kept_bins[which]
        total = end_c(which)
        for q in range(blocks):
            columns = slice(q * 128, q * 128 + 128)
            far_ref[first : first + many, columns] = (
                far_ref[first : first + many, columns] + (total[q] * scale)[0:many]
            )


def store_kernel(e_ref, far_ref, eout_ref, fout_ref, sem):
    bins = far_ref.shape[0]
    stores = [pltpu.make_async_copy(e_ref, eout_ref, sem.at[bins])] + [
        pltpu.make_async_copy(far_ref.at[b : b + 1], fout_ref.at[b], sem.at[b]) for b in range(bins)
    ]
    for store in stores:
        store.start()
    for store in stores:
        store.wait()


def up8(n):
    return (n + 7) // 8 * 8


def local(sizes, initial_field, inv_permittivity, history, tile_rows, owners, delays, weights):
    n_x, n_y, n_z = sizes
    sx, sy, sz = inv_permittivity.shape
    tiles, hpast, width = history.shape
    cap = max(2, 2 * tiles // n_x)
    slots = n_x * cap
    members = n_y * n_z
    plane_n = n_y * (n_z // 2)
    directions = weights.shape[1]
    share = directions // members
    dims = (n_x, n_y, n_z, sx, sy, sz, tiles, hpast, cap, share)
    kept_bins = (hpast + LAG - 1, STEPS - 1 + LAG - 1, LAG)
    anywhere, resident = pl.BlockSpec(memory_space=pl.ANY), pl.BlockSpec(memory_space=pltpu.VMEM)
    f32, bf16 = jnp.float32, jnp.bfloat16
    vmem = pltpu.VMEM
    faces = lambda in_x, in_y: [
        vmem((STEPS, in_x, sy, sz), f32), vmem((STEPS, in_y, sx, sz), f32), vmem((STEPS, sy, sz), f32)
    ]
    rows8 = vmem((STEPS, 8, sz), f32)
    edges = [rows8, rows8] + [vmem((STEPS, sx, sz), f32)] * 2 + [rows8, rows8]
    below = [vmem((2, sy, sz), f32), vmem((2, sx, sz), f32), vmem((2, sy, sz), f32)]
    per_set = lambda make: [make(up8(n_x * bins), up8(bins)) for bins in kept_bins]
    scratch = (
        [vmem((3, sx, sy, sz), f32), vmem((sx, sy, sz), f32)]
        + [vmem((hpast, tiles, width), bf16), vmem((1, tiles), jnp.int32), vmem((1, tiles), jnp.int32)]
        + [vmem(delays.shape, jnp.int32), vmem(weights.shape, bf16)]
        + faces(2, 2)
        + faces(2, 3)
        + [rows8, rows8]
        + faces(2, 2)
        + faces(2, 3)
        + edges
        + below
        + [
            vmem((hpast * slots, width), bf16),
            vmem((STEPS * slots, width), bf16),
            vmem((slots, directions), f32),
            vmem((2, hpast * slots, share // 2), f32),
            vmem((2, slots, share), f32),
        ]
        + per_set(lambda rows, one: vmem((members, share // 128, rows, 128), f32))
        + per_set(lambda rows, one: vmem((plane_n, share // 128, rows, 128), f32))
        + per_set(lambda rows, one: vmem((plane_n, share // 128, rows, 128), f32))
        + per_set(lambda rows, one: vmem((plane_n, share // 128, rows, 128), f32))
        + per_set(lambda rows, one: vmem((share // 128, rows, 128), f32))
        + per_set(lambda rows, one: vmem((n_x, share // 128, one, 128), f32))
        + per_set(lambda rows, one: vmem((n_x, share // 128, one, 128), f32))
        + [pltpu.SemaphoreType.DMA((12,)), pltpu.SemaphoreType.DMA((2, 12))]
        + [pltpu.SemaphoreType.DMA((plane_n,)), pltpu.SemaphoreType.DMA((2, plane_n))]
        + [pltpu.SemaphoreType.DMA((plane_n - 1,)), pltpu.SemaphoreType.DMA((4, plane_n - 1))]
        + [pltpu.SemaphoreType.DMA((n_x - 1,)), pltpu.SemaphoreType.DMA((3, n_x - 1))]
        + [pltpu.SemaphoreType.DMA((7,))]
    )
    efield, far = pl.pallas_call(
        functools.partial(kernel, dims),
        out_shape=(vmem(initial_field.shape, f32), vmem((NB, share), f32)),
        in_specs=[anywhere] * 7,
        out_specs=(resident, resident),
        scratch_shapes=scratch,
        compiler_params=pltpu.CompilerParams(
            collective_id=0, has_side_effects=True, vmem_limit_bytes=56 * 1024 * 1024
        ),
    )(
        initial_field, inv_permittivity, jnp.transpose(history, (1, 0, 2)),
        tile_rows[None], owners.reshape(1, tiles), delays, weights,
    )
    efield = pltpu.with_memory_space_constraint(efield, pltpu.VMEM)
    far = pltpu.with_memory_space_constraint(far, pltpu.VMEM)
    efield, far = pl.pallas_call(
        store_kernel,
        out_shape=(
            jax.ShapeDtypeStruct(initial_field.shape, f32), jax.ShapeDtypeStruct((NB, 1, share), f32)
        ),
        in_specs=[resident, resident],
        out_specs=(anywhere, anywhere),
        scratch_shapes=[pltpu.SemaphoreType.DMA((NB + 1,))],
    )(efield, far)
    return efield, jnp.transpose(far, (1, 0, 2))


def solution(mesh):
    placed = (
        P(None, "gx", "gy", "gz"),
        P("gx", "gy", "gz"),
        P(("gx", "gy", "gz"), None, None),
        P(("gx", "gy", "gz")),
        P(("gx", "gy", "gz"), None),
        P(("gx", "gy", "gz"), None),
        P(),
    )
    sizes = (mesh.shape["gx"], mesh.shape["gy"], mesh.shape["gz"])
    return jax.shard_map(
        functools.partial(local, sizes),
        mesh=mesh,
        in_specs=placed,
        out_specs=(P(None, "gx", "gy", "gz"), P("gx", None, ("gy", "gz"))),
        check_vma=False,
    )
```
